128 devices in a mesh: gx: 4 (over x), gy: 4 (over y), gz: 8 (over z, core).
Axes of the slice: x: 4, y: 4, z: 4, core: 2. Of those that a mesh axis runs over, the one named last changes fastest.
Arguments:
- orbitals: float32 [4, 256, 256, 1024], P(None, 'gx', 'gy', 'gz'), may hold values from -6 to 6
- potential: float32 [256, 256, 1024], P('gx', 'gy', 'gz'), may hold values from -2 to 0
Outputs:
- basis: float32 [4, 256, 256, 1024], P(None, 'gx', 'gy', 'gz')
- factor: float32 [4, 4], replicated
The draws below stay inside these ranges and needn't reach their ends.
All inputs are finite; a program needn't handle non-finite values.
Results may differ from the reference program's by a relative error of at most 0.00011.
Values sent between devices are 32-bit elements; how exact they have to be, the bound alone decides.
A program may use at most 256 MiB of HBM per device.

```python
import jax
import jax.numpy as jnp
from jax import lax

NORB = 4
NX = 256
NY = 256
NZ = 1024


def shard_levels(own_key, shape, shards, least, largest):
    gain, own = 1.0, jax.random.fold_in(own_key, 6)
    for position, blocks in shards:
        steps = jnp.exp(jax.random.uniform(jax.random.fold_in(own, position), (blocks,), jnp.float32, least / len(shards), largest / len(shards)))
        gain = gain * jnp.repeat(steps, shape[position] // blocks).reshape([-1 if axis == position else 1 for axis in range(len(shape))])
    return gain


def bell_draw(key, shape, scale, bound, cuts=(), kind=jnp.bfloat16):
    values = scale * jax.random.normal(key, shape, jnp.float32)
    if cuts:
        values = values * shard_levels(key, shape, cuts, -0.22, 0.18)
    return jnp.clip(values, -bound, bound).astype(kind)


def setup_inputs(seed: int = 0) -> dict:
    keys = jax.random.split(jax.random.key(seed), 3)
    orbitals = bell_draw(keys[0], (NORB, NX, NY, NZ), 1.0, 6.0, ((1, 4), (2, 4), (3, 8)), jnp.float32)
    potential = jnp.clip(-2.0 + 2.0 * jax.random.uniform(keys[1], (NX, NY, NZ), jnp.float32) ** shard_levels(keys[1], (NX, NY, NZ), ((0, 4), (1, 4), (2, 8)), -0.2, 0.2), -2.0, 0.0)
    return {"orbitals": orbitals, "potential": potential}


def shifted(padded, axis, offset):
    pieces = []
    for which in range(3):
        length = padded.shape[which - 3]
        if which - 3 == axis:
            pieces.append(slice(2 + offset, length - 2 + offset))
        else:
            pieces.append(slice(2, length - 2))
    return padded[..., pieces[0], pieces[1], pieces[2]]

def kinetic(padded):
    total = -7.5 * shifted(padded, -1, 0)
    for axis in (-3, -2, -1):
        for offset, weight in ((1, 4.0 / 3.0), (2, -1.0 / 12.0)):
            total = total + weight * (shifted(padded, axis, offset) + shifted(padded, axis, -offset))
    return -0.5 * total

def apply_hamiltonian(field, potential):
    padded = jnp.pad(field, ((0, 0), (2, 2), (2, 2), (2, 2)))
    return kinetic(padded) + potential[None] * field

def reference(orbitals, potential):
    centre = 4.5
    half_width = 3.5
    level_zero = orbitals
    level_one = (apply_hamiltonian(level_zero, potential) - centre * level_zero) / half_width
    level_two = 2.0 * (apply_hamiltonian(level_one, potential) - centre * level_one) / half_width - level_zero
    filtered = 2.0 * (apply_hamiltonian(level_two, potential) - centre * level_two) / half_width - level_one
    gram = jnp.einsum('iabc,jabc->ij', filtered, filtered, precision=lax.Precision.HIGHEST) / (NX * NY * NZ)
    factor = jnp.linalg.cholesky(gram).T
    inverse = jax.scipy.linalg.solve_triangular(factor, jnp.eye(NORB, dtype=factor.dtype), lower=False)
    basis = jnp.einsum('ij,iabc->jabc', inverse, filtered, precision=lax.Precision.HIGHEST)
    return (basis, factor)
```

```python
import functools

import jax
import jax.numpy as jnp
from jax import lax
from jax.experimental import pallas as pl
from jax.experimental.pallas import tpu as pltpu
from jax.sharding import PartitionSpec as P

MESH = pl.DeviceIdType.MESH
LANES = 128
SLAB = 8
ROW0 = 8


def merge(tree, value, lane):
    size = 0
    while tree and tree[-1][0] == size:
        width, low = tree.pop()
        start, span = 2, 4 << size
        start = 2 + 4 * ((1 << size) - 1)
        value = jnp.where(
            (lane >= start) & (lane < start + span), pltpu.roll(value, span, 1), low
        )
        size += 1
    tree.append((size, value))


def packed(tree):
    return pltpu.roll(tree[0][1], 2, 1)


def filter_kernel(
    sizes, orb, pot, out, gram, u, q, own, zin, ecor, acc, g0, g1, g2,
    load_sem, pot_sem, xs, xr, ys, yr, zs, zr, g0s, g0r, g1s, g1r, g2s, g2r,
):
    nx, ny, cx, cy, cz = sizes
    slabs = nx // SLAB
    blocks = ny // 8
    groups = blocks // 4
    orbs = 4
    gx, gy, gz = lax.axis_index("gx"), lax.axis_index("gy"), lax.axis_index("gz")
    here = [gx, gy, gz]
    counts = [cx, cy, cz]

    def device(axis, index):
        return tuple(index if a == axis else here[a] for a in range(3))

    def load(s):
        x0 = s * SLAB
        return (
            pltpu.make_async_copy(
                orb.at[:, pl.ds(x0, SLAB)],
                u.at[0, :, pl.ds(2 + x0, SLAB), pl.ds(ROW0, ny)],
                load_sem.at[s],
            ),
            pltpu.make_async_copy(
                pot.at[pl.ds(x0, SLAB)], q.at[pl.ds(x0, SLAB)], pot_sem.at[s]
            ),
        )

    @pl.loop(0, slabs)
    def _(i):
        for copy in load(lax.rem(i + 1, slabs)):
            copy.start()

    barrier = pltpu.get_barrier_semaphore()
    for axis in range(3):
        for k in range(1, counts[axis]):
            peer = lax.rem(here[axis] + k, counts[axis])
            pl.semaphore_signal(
                barrier, inc=1, device_id=device(axis, peer), device_id_type=MESH
            )
    pl.semaphore_wait(barrier, cx + cy + cz - 3)

    def x_copy(level, side):
        buf = level % 2
        first = nx if side == 0 else 2
        target = 0 if side == 0 else nx + 2
        if level == 0:
            source = orb.at[:, pl.ds(first - 2, 2)]
        else:
            source = u.at[buf, :, pl.ds(first, 2), pl.ds(ROW0, ny)]
        return pltpu.make_async_remote_copy(
            src_ref=source,
            dst_ref=u.at[buf, :, pl.ds(target, 2), pl.ds(ROW0, ny)],
            send_sem=xs.at[level, side],
            recv_sem=xr.at[level, side],
            device_id=device(0, gx + 1 if side == 0 else gx - 1),
            device_id_type=MESH,
        )

    def y_copy(level, side, s):
        buf = level % 2
        planes = pl.ds(2 + s * SLAB, SLAB)
        first = ROW0 + ny - 2 if side == 0 else ROW0
        target = ROW0 - 2 if side == 0 else ROW0 + ny
        return pltpu.make_async_remote_copy(
            src_ref=u.at[buf, :, planes, pl.ds(first, 2)],
            dst_ref=u.at[buf, :, planes, pl.ds(target, 2)],
            send_sem=ys.at[level, side, s],
            recv_sem=yr.at[level, side, s],
            device_id=device(1, gy + 1 if side == 0 else gy - 1),
            device_id_type=MESH,
        )

    def z_copy(level, side, s):
        return pltpu.make_async_remote_copy(
            src_ref=own.at[level, s],
            dst_ref=zin.at[level, side, s],
            send_sem=zs.at[level, side, s],
            recv_sem=zr.at[level, side, s],
            device_id=device(2, gz + 1 if side == 0 else gz - 1),
            device_id_type=MESH,
        )

    def sends(axis, side):
        return here[axis] < counts[axis] - 1 if side == 0 else here[axis] > 0

    def receives(axis, side):
        return here[axis] > 0 if side == 0 else here[axis] < counts[axis] - 1

    def send_slab(level, s):
        for side in range(2):

            @pl.when(sends(1, side))
            def _():
                y_copy(level, side, s).start()

            @pl.when(sends(2, side))
            def _():
                z_copy(level, side, s).start()

    for side in range(2):

        @pl.when(sends(0, side))
        def _():
            x_copy(0, side).start()

    for side in range(2):
        xt = 0 if side == 0 else nx + 2
        yt = ROW0 - 2 if side == 0 else ROW0 + ny

        @pl.when(jnp.logical_not(receives(0, side)))
        def _():
            @pl.loop(0, orbs)
            def _(o):
                for buf in range(2):
                    for plane in range(2):
                        u[buf, o, xt + plane, ROW0 : ROW0 + ny, :] = jnp.zeros(
                            (ny, LANES), jnp.float32
                        )

        @pl.when(jnp.logical_not(receives(1, side)))
        def _():
            @pl.loop(0, orbs)
            def _(o):
                @pl.loop(2, nx + 2)
                def _(x):
                    for buf in range(2):
                        u[buf, o, x, yt : yt + 2, :] = jnp.zeros((2, LANES), jnp.float32)

        @pl.when(jnp.logical_not(receives(2, side)))
        def _():
            @pl.loop(0, slabs)
            def _(s):
                for level in range(3):
                    zin[level, side, s] = jnp.zeros((orbs, groups, 8, LANES), jnp.float32)

    lane = lax.broadcasted_iota(jnp.int32, (8, LANES), 1)
    phase = lane & 3
    edge = (lane < 2) | (lane >= LANES - 2)

    @pl.loop(0, slabs)
    def _(i):
        s = lax.rem(i + 1, slabs)
        x0 = s * SLAB
        for copy in load(s):
            copy.wait()

        @pl.loop(0, orbs)
        def _(o):
            for g in range(groups):
                tree = []
                for b in range(4):
                    y = ROW0 + 8 * (4 * g + b)
                    for x in range(SLAB):
                        merge(tree, u[0, o, x0 + 2 + x, y : y + 8, :], lane)
                own[0, s, o, g] = packed(tree)

        send_slab(0, s)

        @pl.loop(0, SLAB)
        def _(x):
            q[x0 + x] = 24.0 * q[x0 + x] - 18.0

    for level in range(3):
        src, dst = level % 2, (level + 1) % 2

        @pl.loop(0, slabs)
        def _(i, level=level, src=src, dst=dst):
            s = lax.rem(i + 1, slabs)
            x0 = s * SLAB
            for side in range(2):

                @pl.when(receives(1, side))
                def _():
                    y_copy(level, side, s).wait_recv()

                @pl.when(receives(2, side))
                def _():
                    z_copy(level, side, s).wait_recv()

                @pl.when(
                    jnp.logical_and(
                        receives(0, side), s == (0 if side == 0 else slabs - 1)
                    )
                )
                def _():
                    x_copy(level, side).wait_recv()

                if level == 1:

                    @pl.when(sends(1, side))
                    def _():
                        y_copy(0, side, s).wait_send()

            @pl.loop(0, orbs)
            def _(o):
                for g in range(groups):
                    delta = (
                        jnp.where(phase < 2, zin[level, 0, s, o, g], zin[level, 1, s, o, g])
                        - own[level, s, o, g]
                    )
                    far = jnp.where(
                        phase < 2,
                        pltpu.roll(delta, LANES - 2, 1),
                        pltpu.roll(delta, 2, 1),
                    )
                    near = jnp.where(
                        phase == 1,
                        pltpu.roll(delta, LANES - 1, 1),
                        jnp.where(phase == 2, pltpu.roll(delta, 1, 1), 0.0),
                    )
                    fix = far - 16.0 * near
                    tree = []
                    for b in range(4):
                        y = ROW0 + 8 * (4 * g + b)
                        c = [u[src, o, x0 + j, y : y + 8, :] for j in range(SLAB + 4)]
                        for x in range(SLAB):
                            k = b * SLAB + x
                            v = c[x + 2]
                            px = x0 + 2 + x

                            def row(d):
                                return u[src, o, px, y + d : y + d + 8, :]

                            one = (c[x + 1] + c[x + 3]) + (row(-1) + row(1))
                            one = one + (pltpu.roll(v, 1, 1) + pltpu.roll(v, LANES - 1, 1))
                            two = (c[x] + c[x + 4]) + (row(-2) + row(2))
                            two = two + (pltpu.roll(v, 2, 1) + pltpu.roll(v, LANES - 2, 1))
                            cor = jnp.where(
                                edge, pltpu.roll(fix, (2 * LANES - 4 * k - 2) % LANES, 1), 0.0
                            )
                            total = (
                                q[x0 + x, y - ROW0 : y - ROW0 + 8, :] * v
                                + (two + cor)
                                - 16.0 * one
                            )
                            if level == 0:
                                new = total * (1.0 / 84.0)
                            else:
                                new = total * (1.0 / 42.0) - u[dst, o, px, y : y + 8, :]
                            if level < 2:
                                u[dst, o, px, y : y + 8, :] = new
                                merge(tree, new, lane)
                            else:
                                out[o, x0 + x, y - ROW0 : y - ROW0 + 8, :] = new
                    if level < 2:
                        own[level + 1, s, o, g] = packed(tree)

            if level < 2:
                send_slab(level + 1, s)
                for side in range(2):

                    @pl.when(
                        jnp.logical_and(sends(0, side), s == (slabs - 1 if side == 0 else 0))
                    )
                    def _():
                        x_copy(level + 1, side).start()

            else:

                @pl.when(i == 0)
                def _():
                    acc[...] = jnp.zeros_like(acc)

                @pl.loop(0, SLAB)
                def _(x):
                    sums = [None] * 10
                    for b in range(blocks):
                        f = [out[o, x0 + x, 8 * b : 8 * b + 8, :] for o in range(orbs)]
                        n = 0
                        for o in range(orbs):
                            for p in range(o, orbs):
                                term = f[o] * f[p]
                                sums[n] = term if sums[n] is None else sums[n] + term
                                n += 1
                    for n in range(10):
                        acc[n] = acc[n] + sums[n]

    total = jnp.concatenate(
        [jnp.sum(acc[n], axis=0, keepdims=True) for n in range(10)]
        + [jnp.zeros((6, LANES), jnp.float32)],
        axis=0,
    )
    for axis, slots, ss, rs in ((2, g0, g0s, g0r), (1, g1, g1s, g1r), (0, g2, g2s, g2r)):
        me, count = here[axis], counts[axis]
        slots[me] = total

        def g_copy(k):
            return pltpu.make_async_remote_copy(
                src_ref=slots.at[me],
                dst_ref=slots.at[me],
                send_sem=ss.at[k],
                recv_sem=rs.at[k],
                device_id=device(axis, lax.rem(me + k, count)),
                device_id_type=MESH,
            )

        def g_arrival(k):
            peer = lax.rem(me + count - k, count)
            return pltpu.make_async_remote_copy(
                src_ref=slots.at[peer],
                dst_ref=slots.at[peer],
                send_sem=ss.at[k],
                recv_sem=rs.at[k],
                device_id=device(axis, peer),
                device_id_type=MESH,
            )

        for k in range(1, count):
            g_copy(k).start()
        for k in range(1, count):
            g_arrival(k).wait_recv()
        total = slots[0]
        for k in range(1, count):
            total = total + slots[k]
        for k in range(1, count):
            g_copy(k).wait_send()
    gram[...] = total

    for level in range(3):
        for side in range(2):

            @pl.when(sends(0, side))
            def _():
                x_copy(level, side).wait_send()

            @pl.loop(0, slabs)
            def _(s):
                if level > 0:

                    @pl.when(sends(1, side))
                    def _():
                        y_copy(level, side, s).wait_send()

                @pl.when(sends(2, side))
                def _():
                    z_copy(level, side, s).wait_send()


def basis_kernel(cells, filtered, gram, basis, factor, inv):
    @pl.when(pl.program_id(0) == 0)
    def _():
        sums = jnp.sum(gram[...], axis=1, keepdims=True) * (1.0 / cells)
        sums = jnp.broadcast_to(sums, (16, LANES))
        g, n = {}, 0
        for i in range(4):
            for j in range(i, 4):
                g[i, j] = sums[n : n + 1, :]
                n += 1
        r = {}
        for i in range(4):
            for j in range(i, 4):
                value = g[i, j]
                for m in range(i):
                    value = value - r[m, i] * r[m, j]
                r[i, j] = jnp.sqrt(value) if i == j else value / r[i, i]
        w = {}
        for j in range(4):
            w[j, j] = 1.0 / r[j, j]
            for i in range(j - 1, -1, -1):
                value = r[i, i + 1] * w[i + 1, j]
                for m in range(i + 2, j + 1):
                    value = value + r[i, m] * w[m, j]
                w[i, j] = -value / r[i, i]
        n = 0
        for i in range(4):
            for j in range(i, 4):
                inv[n] = jnp.broadcast_to(w[i, j], (8, LANES))
                n += 1
        line = lax.broadcasted_iota(jnp.int32, (4, 4), 0)
        column = lax.broadcasted_iota(jnp.int32, (4, 4), 1)
        table = jnp.zeros((4, 4), jnp.float32)
        for i in range(4):
            for j in range(i, 4):
                table = jnp.where(
                    (line == i) & (column == j), jnp.broadcast_to(r[i, j][:, :4], (4, 4)), table
                )
        factor[...] = table

    w, n = {}, 0
    for i in range(4):
        for j in range(i, 4):
            w[i, j] = inv[n]
            n += 1
    planes, ny = basis.shape[1], basis.shape[2]

    @pl.loop(0, planes)
    def _(x):
        for b in range(ny // 8):
            f = [filtered[o, x, 8 * b : 8 * b + 8, :] for o in range(4)]
            for j in range(4):
                value = f[0] * w[0, j]
                for i in range(1, j + 1):
                    value = value + f[i] * w[i, j]
                basis[j, x, 8 * b : 8 * b + 8, :] = value


def body(orbitals, potential):
    orbs, nx, ny, nz = orbitals.shape
    cx, cy, cz = (lax.axis_size(a) for a in ("gx", "gy", "gz"))
    slabs, groups = nx // SLAB, ny // 32
    dma = pltpu.SemaphoreType.DMA
    f32 = jnp.float32
    filtered, gram = pl.pallas_call(
        functools.partial(filter_kernel, (nx, ny, cx, cy, cz)),
        out_shape=(
            jax.ShapeDtypeStruct(orbitals.shape, f32),
            jax.ShapeDtypeStruct((16, LANES), f32),
        ),
        in_specs=[pl.BlockSpec(memory_space=pl.ANY)] * 2,
        out_specs=(
            pl.BlockSpec(memory_space=pltpu.VMEM),
            pl.BlockSpec(memory_space=pltpu.VMEM),
        ),
        scratch_shapes=[
            pltpu.VMEM((2, orbs, nx + 4, ny + 16, nz), f32),
            pltpu.VMEM((nx, ny, nz), f32),
            pltpu.VMEM((3, slabs, orbs, groups, 8, LANES), f32),
            pltpu.VMEM((3, 2, slabs, orbs, groups, 8, LANES), f32),
            pltpu.VMEM((8, LANES), f32),
            pltpu.VMEM((10, 8, LANES), f32),
            pltpu.VMEM((cz, 16, LANES), f32),
            pltpu.VMEM((cy, 16, LANES), f32),
            pltpu.VMEM((cx, 16, LANES), f32),
            dma((slabs,)),
            dma((slabs,)),
            dma((3, 2)),
            dma((3, 2)),
            dma((3, 2, slabs)),
            dma((3, 2, slabs)),
            dma((3, 2, slabs)),
            dma((3, 2, slabs)),
            dma((cz,)),
            dma((cz,)),
            dma((cy,)),
            dma((cy,)),
            dma((cx,)),
            dma((cx,)),
        ],
        compiler_params=pltpu.CompilerParams(
            collective_id=0, has_side_effects=True, vmem_limit_bytes=48 << 20
        ),
    )(orbitals, potential)
    planes = 4
    basis, factor = pl.pallas_call(
        functools.partial(basis_kernel, nx * cx * ny * cy * nz * cz),
        grid=(nx // planes,),
        out_shape=(
            jax.ShapeDtypeStruct(orbitals.shape, f32),
            jax.ShapeDtypeStruct((4, 4), f32),
        ),
        in_specs=[
            pl.BlockSpec((orbs, planes, ny, nz), lambda i: (0, i, 0, 0)),
            pl.BlockSpec((16, LANES), lambda i: (0, 0)),
        ],
        out_specs=(
            pl.BlockSpec((orbs, planes, ny, nz), lambda i: (0, i, 0, 0)),
            pl.BlockSpec((4, 4), lambda i: (0, 0)),
        ),
        scratch_shapes=[pltpu.VMEM((10, 8, LANES), f32)],
    )(filtered, gram)
    return basis, factor


def solution(mesh):
    return jax.shard_map(
        body,
        mesh=mesh,
        in_specs=(P(None, "gx", "gy", "gz"), P("gx", "gy", "gz")),
        out_specs=(P(None, "gx", "gy", "gz"), P()),
        check_vma=False,
    )
```

```python
import functools

import jax
import jax.numpy as jnp
from jax import lax
from jax.experimental import pallas as pl
from jax.experimental.pallas import tpu as pltpu
from jax.sharding import PartitionSpec as P

MESH = pl.DeviceIdType.MESH
LANES = 128
SLAB = 8
ROW0 = 8


def merge(tree, value, lane):
    size = 0
    while tree and tree[-1][0] == size:
        low = tree.pop()[1]
        value = jnp.where((lane & (4 << size)) != 0, value, low)
        size += 1
    tree.append((size, value))


def halves(rows):
    parts = []
    for k in range(0, len(rows), 2):
        pair = jnp.concatenate(rows[k : k + 2], axis=0)
        high = pair.astype(jnp.bfloat16)
        low = (pair - high.astype(jnp.float32)).astype(jnp.bfloat16)
        parts.append(jnp.concatenate([high, low], axis=1))
    return jnp.concatenate(parts, axis=0)


def filter_kernel(
    sizes, orb, pot, out, gram, u, q, zp, half, weights, own, zin, acc, g0, g1, g2,
    load_sem, pot_sem, xs, xr, ys, yr, zs, zr, g0s, g0r, g1s, g1r, g2s, g2r,
):
    nx, ny, cx, cy, cz = sizes
    slabs = nx // SLAB
    blocks = ny // 8
    groups = blocks // 4
    orbs = 4
    gx, gy, gz = lax.axis_index("gx"), lax.axis_index("gy"), lax.axis_index("gz")
    here = [gx, gy, gz]
    counts = [cx, cy, cz]

    def device(axis, index):
        return tuple(index if a == axis else here[a] for a in range(3))

    def load(s):
        x0 = s * SLAB
        return (
            pltpu.make_async_copy(
                orb.at[:, pl.ds(x0, SLAB)],
                u.at[0, :, pl.ds(2 + x0, SLAB), pl.ds(ROW0, ny)],
                load_sem.at[s],
            ),
            pltpu.make_async_copy(
                pot.at[pl.ds(x0, SLAB)], q.at[pl.ds(x0, SLAB)], pot_sem.at[s]
            ),
        )

    @pl.loop(0, slabs)
    def _(i):
        for copy in load(lax.rem(i + 1, slabs)):
            copy.start()

    barrier = pltpu.get_barrier_semaphore()
    for axis in range(3):
        for k in range(1, counts[axis]):
            peer = lax.rem(here[axis] + k, counts[axis])
            pl.semaphore_signal(
                barrier, inc=1, device_id=device(axis, peer), device_id_type=MESH
            )
    pl.semaphore_wait(barrier, cx + cy + cz - 3)

    def x_copy(level, side):
        buf = level % 2
        first = nx if side == 0 else 2
        target = 0 if side == 0 else nx + 2
        if level == 0:
            source = orb.at[:, pl.ds(first - 2, 2)]
        else:
            source = u.at[buf, :, pl.ds(first, 2), pl.ds(ROW0, ny)]
        return pltpu.make_async_remote_copy(
            src_ref=source,
            dst_ref=u.at[buf, :, pl.ds(target, 2), pl.ds(ROW0, ny)],
            send_sem=xs.at[level, side],
            recv_sem=xr.at[level, side],
            device_id=device(0, gx + 1 if side == 0 else gx - 1),
            device_id_type=MESH,
        )

    def y_copy(level, side, s):
        buf = level % 2
        planes = pl.ds(2 + s * SLAB, SLAB)
        first = ROW0 + ny - 2 if side == 0 else ROW0
        target = ROW0 - 2 if side == 0 else ROW0 + ny
        return pltpu.make_async_remote_copy(
            src_ref=u.at[buf, :, planes, pl.ds(first, 2)],
            dst_ref=u.at[buf, :, planes, pl.ds(target, 2)],
            send_sem=ys.at[level, side, s],
            recv_sem=yr.at[level, side, s],
            device_id=device(1, gy + 1 if side == 0 else gy - 1),
            device_id_type=MESH,
        )

    def z_copy(level, side, s):
        return pltpu.make_async_remote_copy(
            src_ref=own.at[level, s],
            dst_ref=zin.at[level, side, s],
            send_sem=zs.at[level, side, s],
            recv_sem=zr.at[level, side, s],
            device_id=device(2, gz + 1 if side == 0 else gz - 1),
            device_id_type=MESH,
        )

    def sends(axis, side):
        return here[axis] < counts[axis] - 1 if side == 0 else here[axis] > 0

    def receives(axis, side):
        return here[axis] > 0 if side == 0 else here[axis] < counts[axis] - 1

    def send_slab(level, s):
        for side in range(2):

            @pl.when(sends(1, side))
            def _():
                y_copy(level, side, s).start()

            @pl.when(sends(2, side))
            def _():
                z_copy(level, side, s).start()

    for side in range(2):

        @pl.when(sends(0, side))
        def _():
            x_copy(0, side).start()

    for side in range(2):
        xt = 0 if side == 0 else nx + 2
        yt = ROW0 - 2 if side == 0 else ROW0 + ny

        @pl.when(jnp.logical_not(receives(0, side)))
        def _():
            @pl.loop(0, orbs)
            def _(o):
                for buf in range(2):
                    for plane in range(2):
                        u[buf, o, xt + plane, ROW0 : ROW0 + ny, :] = jnp.zeros(
                            (ny, LANES), jnp.float32
                        )

        @pl.when(jnp.logical_not(receives(1, side)))
        def _():
            @pl.loop(0, orbs)
            def _(o):
                @pl.loop(2, nx + 2)
                def _(x):
                    for buf in range(2):
                        u[buf, o, x, yt : yt + 2, :] = jnp.zeros((2, LANES), jnp.float32)

        @pl.when(jnp.logical_not(receives(2, side)))
        def _():
            @pl.loop(0, slabs)
            def _(s):
                for level in range(3):
                    zin[level, side, s] = jnp.zeros((orbs, groups, 8, LANES), jnp.float32)

    lane = lax.broadcasted_iota(jnp.int32, (8, LANES), 1)
    phase = lane & 3
    edge = (lane < 2) | (lane >= LANES - 2)

    source = lax.broadcasted_iota(jnp.int32, (2 * LANES, 2 * LANES), 0) & (LANES - 1)
    target = lax.broadcasted_iota(jnp.int32, (2 * LANES, 2 * LANES), 1)
    step = (target - source) & (LANES - 1)
    band = jnp.where(
        (step == 1) | (step == LANES - 1),
        -16.0,
        jnp.where((step == 2) | (step == LANES - 2), 1.0, 0.0),
    )
    ends = jnp.where((target & 3) == ((source + 2) & (LANES - 1)), 1.0, 0.0)
    weights[...] = jnp.where(target < LANES, band, ends).astype(jnp.bfloat16)

    def along_z(level, s, o):
        done = jnp.dot(half[...], weights[...], preferred_element_type=jnp.float32)
        for g in range(groups):
            tree = []
            for b in range(4 * g, 4 * g + 4):
                for x in range(SLAB):
                    row = 8 * (b * SLAB + x)
                    zp[o, s * SLAB + x, 8 * b : 8 * b + 8, :] = done[row : row + 8, :LANES]
                    merge(tree, done[row : row + 8, LANES:], lane)
            own[level, s, o, g] = tree[0][1]

    @pl.loop(0, slabs)
    def _(i):
        s = lax.rem(i + 1, slabs)
        x0 = s * SLAB
        for copy in load(s):
            copy.wait()

        @pl.loop(0, orbs)
        def _(o):
            for b in range(blocks):
                y = ROW0 + 8 * b
                half[SLAB * 8 * b : SLAB * 8 * (b + 1), :] = halves(
                    [u[0, o, x0 + 2 + x, y : y + 8, :] for x in range(SLAB)]
                )
            along_z(0, s, o)

        send_slab(0, s)

        @pl.loop(0, SLAB)
        def _(x):
            q[x0 + x] = 24.0 * q[x0 + x] - 18.0

    for level in range(3):
        src, dst = level % 2, (level + 1) % 2

        @pl.loop(0, slabs)
        def _(i, level=level, src=src, dst=dst):
            s = lax.rem(i + 1, slabs)
            x0 = s * SLAB
            for side in range(2):

                @pl.when(receives(1, side))
                def _():
                    y_copy(level, side, s).wait_recv()

                @pl.when(receives(2, side))
                def _():
                    z_copy(level, side, s).wait_recv()

                @pl.when(
                    jnp.logical_and(
                        receives(0, side), s == (0 if side == 0 else slabs - 1)
                    )
                )
                def _():
                    x_copy(level, side).wait_recv()

                if level == 1:

                    @pl.when(sends(1, side))
                    def _():
                        y_copy(0, side, s).wait_send()

            @pl.loop(0, orbs)
            def _(o):
                for g in range(groups):
                    delta = (
                        jnp.where(phase < 2, zin[level, 0, s, o, g], zin[level, 1, s, o, g])
                        - own[level, s, o, g]
                    )
                    far = jnp.where(
                        phase < 2,
                        pltpu.roll(delta, LANES - 2, 1),
                        pltpu.roll(delta, 2, 1),
                    )
                    near = jnp.where(
                        phase == 1,
                        pltpu.roll(delta, LANES - 1, 1),
                        jnp.where(phase == 2, pltpu.roll(delta, 1, 1), 0.0),
                    )
                    fix = far - 16.0 * near
                    for b in range(4):
                        y = ROW0 + 8 * (4 * g + b)
                        c = [u[src, o, x0 + j, y : y + 8, :] for j in range(SLAB + 4)]
                        news = []
                        for x in range(SLAB):
                            k = b * SLAB + x
                            v = c[x + 2]
                            px = x0 + 2 + x

                            def row(d):
                                return u[src, o, px, y + d : y + d + 8, :]

                            one = (c[x + 1] + c[x + 3]) + (row(-1) + row(1))
                            two = (c[x] + c[x + 4]) + (row(-2) + row(2))
                            cor = jnp.where(
                                edge, pltpu.roll(fix, (2 * LANES - 4 * k - 2) % LANES, 1), 0.0
                            )
                            total = (
                                q[x0 + x, y - ROW0 : y - ROW0 + 8, :] * v
                                + (zp[o, x0 + x, y - ROW0 : y - ROW0 + 8, :] + cor)
                                + two
                                - 16.0 * one
                            )
                            if level == 0:
                                new = total * (1.0 / 84.0)
                            else:
                                new = total * (1.0 / 42.0) - u[dst, o, px, y : y + 8, :]
                            if level < 2:
                                u[dst, o, px, y : y + 8, :] = new
                                news.append(new)
                            else:
                                out[o, x0 + x, y - ROW0 : y - ROW0 + 8, :] = new
                        if level < 2:
                            row = SLAB * (y - ROW0)
                            half[row : row + 8 * SLAB, :] = halves(news)
                if level < 2:
                    along_z(level + 1, s, o)

            if level < 2:
                send_slab(level + 1, s)
                for side in range(2):

                    @pl.when(
                        jnp.logical_and(sends(0, side), s == (slabs - 1 if side == 0 else 0))
                    )
                    def _():
                        x_copy(level + 1, side).start()

            else:

                @pl.when(i == 0)
                def _():
                    acc[...] = jnp.zeros_like(acc)

                @pl.loop(0, SLAB)
                def _(x):
                    sums = [None] * 10
                    for b in range(blocks):
                        f = [out[o, x0 + x, 8 * b : 8 * b + 8, :] for o in range(orbs)]
                        n = 0
                        for o in range(orbs):
                            for p in range(o, orbs):
                                term = f[o] * f[p]
                                sums[n] = term if sums[n] is None else sums[n] + term
                                n += 1
                    for n in range(10):
                        acc[n] = acc[n] + sums[n]

    total = jnp.concatenate(
        [jnp.sum(acc[n], axis=0, keepdims=True) for n in range(10)]
        + [jnp.zeros((6, LANES), jnp.float32)],
        axis=0,
    )
    for axis, slots, ss, rs in ((2, g0, g0s, g0r), (1, g1, g1s, g1r), (0, g2, g2s, g2r)):
        me, count = here[axis], counts[axis]
        slots[me] = total

        def g_copy(k):
            return pltpu.make_async_remote_copy(
                src_ref=slots.at[me],
                dst_ref=slots.at[me],
                send_sem=ss.at[k],
                recv_sem=rs.at[k],
                device_id=device(axis, lax.rem(me + k, count)),
                device_id_type=MESH,
            )

        def g_arrival(k):
            peer = lax.rem(me + count - k, count)
            return pltpu.make_async_remote_copy(
                src_ref=slots.at[peer],
                dst_ref=slots.at[peer],
                send_sem=ss.at[k],
                recv_sem=rs.at[k],
                device_id=device(axis, peer),
                device_id_type=MESH,
            )

        for k in range(1, count):
            g_copy(k).start()
        for k in range(1, count):
            g_arrival(k).wait_recv()
        total = slots[0]
        for k in range(1, count):
            total = total + slots[k]
        for k in range(1, count):
            g_copy(k).wait_send()
    gram[...] = total

    for level in range(3):
        for side in range(2):

            @pl.when(sends(0, side))
            def _():
                x_copy(level, side).wait_send()

            @pl.loop(0, slabs)
            def _(s):
                if level > 0:

                    @pl.when(sends(1, side))
                    def _():
                        y_copy(level, side, s).wait_send()

                @pl.when(sends(2, side))
                def _():
                    z_copy(level, side, s).wait_send()


def basis_kernel(cells, filtered, gram, basis, factor, inv):
    @pl.when(pl.program_id(0) == 0)
    def _():
        sums = jnp.sum(gram[...], axis=1, keepdims=True) * (1.0 / cells)
        sums = jnp.broadcast_to(sums, (16, LANES))
        g, n = {}, 0
        for i in range(4):
            for j in range(i, 4):
                g[i, j] = sums[n : n + 1, :]
                n += 1
        r = {}
        for i in range(4):
            for j in range(i, 4):
                value = g[i, j]
                for m in range(i):
                    value = value - r[m, i] * r[m, j]
                r[i, j] = jnp.sqrt(value) if i == j else value / r[i, i]
        w = {}
        for j in range(4):
            w[j, j] = 1.0 / r[j, j]
            for i in range(j - 1, -1, -1):
                value = r[i, i + 1] * w[i + 1, j]
                for m in range(i + 2, j + 1):
                    value = value + r[i, m] * w[m, j]
                w[i, j] = -value / r[i, i]
        n = 0
        for i in range(4):
            for j in range(i, 4):
                inv[n] = jnp.broadcast_to(w[i, j], (8, LANES))
                n += 1
        line = lax.broadcasted_iota(jnp.int32, (4, 4), 0)
        column = lax.broadcasted_iota(jnp.int32, (4, 4), 1)
        table = jnp.zeros((4, 4), jnp.float32)
        for i in range(4):
            for j in range(i, 4):
                table = jnp.where(
                    (line == i) & (column == j), jnp.broadcast_to(r[i, j][:, :4], (4, 4)), table
                )
        factor[...] = table

    w, n = {}, 0
    for i in range(4):
        for j in range(i, 4):
            w[i, j] = inv[n]
            n += 1
    planes, ny = basis.shape[1], basis.shape[2]
    x0 = pl.program_id(0) * planes

    @pl.loop(0, planes)
    def _(x):
        for b in range(ny // 8):
            f = [filtered[o, x0 + x, 8 * b : 8 * b + 8, :] for o in range(4)]
            for j in range(4):
                value = f[0] * w[0, j]
                for i in range(1, j + 1):
                    value = value + f[i] * w[i, j]
                basis[j, x, 8 * b : 8 * b + 8, :] = value


def body(orbitals, potential):
    orbs, nx, ny, nz = orbitals.shape
    cx, cy, cz = (lax.axis_size(a) for a in ("gx", "gy", "gz"))
    slabs, groups = nx // SLAB, ny // 32
    dma = pltpu.SemaphoreType.DMA
    f32 = jnp.float32
    filtered, gram = pl.pallas_call(
        functools.partial(filter_kernel, (nx, ny, cx, cy, cz)),
        out_shape=(
            pltpu.VMEM(orbitals.shape, f32),
            pltpu.VMEM((16, LANES), f32),
        ),
        in_specs=[pl.BlockSpec(memory_space=pl.ANY)] * 2,
        out_specs=(
            pl.BlockSpec(memory_space=pltpu.VMEM),
            pl.BlockSpec(memory_space=pltpu.VMEM),
        ),
        scratch_shapes=[
            pltpu.VMEM((2, orbs, nx + 4, ny + 16, nz), f32),
            pltpu.VMEM((nx, ny, nz), f32),
            pltpu.VMEM((orbs, nx, ny, nz), f32),
            pltpu.VMEM((SLAB * ny, 2 * nz), jnp.bfloat16),
            pltpu.VMEM((2 * nz, 2 * nz), jnp.bfloat16),
            pltpu.VMEM((3, slabs, orbs, groups, 8, LANES), f32),
            pltpu.VMEM((3, 2, slabs, orbs, groups, 8, LANES), f32),
            pltpu.VMEM((10, 8, LANES), f32),
            pltpu.VMEM((cz, 16, LANES), f32),
            pltpu.VMEM((cy, 16, LANES), f32),
            pltpu.VMEM((cx, 16, LANES), f32),
            dma((slabs,)),
            dma((slabs,)),
            dma((3, 2)),
            dma((3, 2)),
            dma((3, 2, slabs)),
            dma((3, 2, slabs)),
            dma((3, 2, slabs)),
            dma((3, 2, slabs)),
            dma((cz,)),
            dma((cz,)),
            dma((cy,)),
            dma((cy,)),
            dma((cx,)),
            dma((cx,)),
        ],
        compiler_params=pltpu.CompilerParams(
            collective_id=0, has_side_effects=True, vmem_limit_bytes=48 << 20
        ),
    )(orbitals, potential)
    planes = 4
    basis, factor = pl.pallas_call(
        functools.partial(basis_kernel, nx * cx * ny * cy * nz * cz),
        grid=(nx // planes,),
        out_shape=(
            jax.ShapeDtypeStruct(orbitals.shape, f32),
            jax.ShapeDtypeStruct((4, 4), f32),
        ),
        in_specs=[
            pl.BlockSpec(memory_space=pltpu.VMEM),
            pl.BlockSpec(memory_space=pltpu.VMEM),
        ],
        out_specs=(
            pl.BlockSpec((orbs, planes, ny, nz), lambda i: (0, i, 0, 0)),
            pl.BlockSpec((4, 4), lambda i: (0, 0)),
        ),
        scratch_shapes=[pltpu.VMEM((10, 8, LANES), f32)],
        compiler_params=pltpu.CompilerParams(vmem_limit_bytes=24 << 20),
    )(
        pltpu.with_memory_space_constraint(filtered, pltpu.VMEM),
        pltpu.with_memory_space_constraint(gram, pltpu.VMEM),
    )
    return basis, factor


def solution(mesh):
    return jax.shard_map(
        body,
        mesh=mesh,
        in_specs=(P(None, "gx", "gy", "gz"), P("gx", "gy", "gz")),
        out_specs=(P(None, "gx", "gy", "gz"), P()),
        check_vma=False,
    )
```

```python
import functools

import jax
import jax.numpy as jnp
from jax import lax
from jax.experimental import pallas as pl
from jax.experimental.pallas import tpu as pltpu
from jax.sharding import PartitionSpec as P

MESH = pl.DeviceIdType.MESH
LANES = 128
SLAB = 8
ROW0 = 8


def merge(tree, value, lane):
    size = 0
    while tree and tree[-1][0] == size:
        low = tree.pop()[1]
        value = jnp.where((lane & (4 << size)) != 0, value, low)
        size += 1
    tree.append((size, value))


def halves(rows):
    parts = []
    for k in range(0, len(rows), 2):
        pair = jnp.concatenate(rows[k : k + 2], axis=0)
        high = pair.astype(jnp.bfloat16)
        low = (pair - high.astype(jnp.float32)).astype(jnp.bfloat16)
        parts.append(jnp.concatenate([high, low], axis=1))
    return jnp.concatenate(parts, axis=0)


def filter_kernel(
    sizes, orb, pot, out, gram, u, q, zp, half, weights, own, zin, acc, g0, g1, g2,
    load_sem, pot_sem, xs, xr, ys, yr, zs, zr, g0s, g0r, g1s, g1r, g2s, g2r,
):
    nx, ny, cx, cy, cz = sizes
    slabs = nx // SLAB
    blocks = ny // 8
    groups = blocks // 4
    orbs = 4
    gx, gy, gz = lax.axis_index("gx"), lax.axis_index("gy"), lax.axis_index("gz")
    here = [gx, gy, gz]
    counts = [cx, cy, cz]

    def device(axis, index):
        return tuple(index if a == axis else here[a] for a in range(3))

    def load(s):
        x0 = s * SLAB
        return (
            pltpu.make_async_copy(
                orb.at[:, pl.ds(x0, SLAB)],
                u.at[0, :, pl.ds(2 + x0, SLAB), pl.ds(ROW0, ny)],
                load_sem.at[s],
            ),
            pltpu.make_async_copy(
                pot.at[pl.ds(x0, SLAB)], q.at[pl.ds(x0, SLAB)], pot_sem.at[s]
            ),
        )

    @pl.loop(0, slabs)
    def _(i):
        for copy in load(lax.rem(i + 1, slabs)):
            copy.start()

    barrier = pltpu.get_barrier_semaphore()
    for axis in range(3):
        for k in range(1, counts[axis]):
            peer = lax.rem(here[axis] + k, counts[axis])
            pl.semaphore_signal(
                barrier, inc=1, device_id=device(axis, peer), device_id_type=MESH
            )
    pl.semaphore_wait(barrier, cx + cy + cz - 3)

    def x_copy(level, side):
        buf = level % 2
        first = nx if side == 0 else 2
        target = 0 if side == 0 else nx + 2
        if level == 0:
            source = orb.at[:, pl.ds(first - 2, 2)]
        else:
            source = u.at[buf, :, pl.ds(first, 2), pl.ds(ROW0, ny)]
        return pltpu.make_async_remote_copy(
            src_ref=source,
            dst_ref=u.at[buf, :, pl.ds(target, 2), pl.ds(ROW0, ny)],
            send_sem=xs.at[level, side],
            recv_sem=xr.at[level, side],
            device_id=device(0, gx + 1 if side == 0 else gx - 1),
            device_id_type=MESH,
        )

    def y_copy(level, side, s):
        buf = level % 2
        planes = pl.ds(2 + s * SLAB, SLAB)
        first = ROW0 + ny - 2 if side == 0 else ROW0
        target = ROW0 - 2 if side == 0 else ROW0 + ny
        return pltpu.make_async_remote_copy(
            src_ref=u.at[buf, :, planes, pl.ds(first, 2)],
            dst_ref=u.at[buf, :, planes, pl.ds(target, 2)],
            send_sem=ys.at[level, side, s],
            recv_sem=yr.at[level, side, s],
            device_id=device(1, gy + 1 if side == 0 else gy - 1),
            device_id_type=MESH,
        )

    def z_copy(level, side, s):
        return pltpu.make_async_remote_copy(
            src_ref=own.at[level, s],
            dst_ref=zin.at[level, side, s],
            send_sem=zs.at[level, side, s],
            recv_sem=zr.at[level, side, s],
            device_id=device(2, gz + 1 if side == 0 else gz - 1),
            device_id_type=MESH,
        )

    def sends(axis, side):
        return here[axis] < counts[axis] - 1 if side == 0 else here[axis] > 0

    def receives(axis, side):
        return here[axis] > 0 if side == 0 else here[axis] < counts[axis] - 1

    def send_slab(level, s):
        for side in range(2):

            @pl.when(sends(1, side))
            def _():
                y_copy(level, side, s).start()

            @pl.when(sends(2, side))
            def _():
                z_copy(level, side, s).start()

    for side in range(2):

        @pl.when(sends(0, side))
        def _():
            x_copy(0, side).start()

    for side in range(2):
        xt = 0 if side == 0 else nx + 2
        yt = ROW0 - 2 if side == 0 else ROW0 + ny

        @pl.when(jnp.logical_not(receives(0, side)))
        def _():
            @pl.loop(0, orbs)
            def _(o):
                for buf in range(2):
                    for plane in range(2):
                        u[buf, o, xt + plane, ROW0 : ROW0 + ny, :] = jnp.zeros(
                            (ny, LANES), jnp.float32
                        )

        @pl.when(jnp.logical_not(receives(1, side)))
        def _():
            @pl.loop(0, orbs)
            def _(o):
                @pl.loop(2, nx + 2)
                def _(x):
                    for buf in range(2):
                        u[buf, o, x, yt : yt + 2, :] = jnp.zeros((2, LANES), jnp.float32)

        @pl.when(jnp.logical_not(receives(2, side)))
        def _():
            @pl.loop(0, slabs)
            def _(s):
                for level in range(3):
                    zin[level, side, s] = jnp.zeros((orbs, groups, 8, LANES), jnp.float32)

    lane = lax.broadcasted_iota(jnp.int32, (8, LANES), 1)
    phase = lane & 3
    edge = (lane < 2) | (lane >= LANES - 2)

    source = lax.broadcasted_iota(jnp.int32, (2 * LANES, 2 * LANES), 0) & (LANES - 1)
    target = lax.broadcasted_iota(jnp.int32, (2 * LANES, 2 * LANES), 1)
    step = (target - source) & (LANES - 1)
    band = jnp.where(
        (step == 1) | (step == LANES - 1),
        -16.0,
        jnp.where((step == 2) | (step == LANES - 2), 1.0, 0.0),
    )
    ends = jnp.where((target & 3) == ((source + 2) & (LANES - 1)), 1.0, 0.0)
    weights[...] = jnp.where(target < LANES, band, ends).astype(jnp.bfloat16)

    def along_z(level, s, o):
        done = jnp.dot(half[o], weights[...], preferred_element_type=jnp.float32)
        for g in range(groups):
            tree = []
            for b in range(4 * g, 4 * g + 4):
                for x in range(SLAB):
                    row = 8 * (b * SLAB + x)
                    zp[o, s * SLAB + x, 8 * b : 8 * b + 8, :] = done[row : row + 8, :LANES]
                    merge(tree, done[row : row + 8, LANES:], lane)
            own[level, s, o, g] = tree[0][1]

    @pl.loop(0, slabs)
    def _(i):
        s = lax.rem(i + 1, slabs)
        x0 = s * SLAB
        for copy in load(s):
            copy.wait()

        for o in range(orbs):
            for b in range(blocks):
                y = ROW0 + 8 * b
                half[o, SLAB * 8 * b : SLAB * 8 * (b + 1), :] = halves(
                    [u[0, o, x0 + 2 + x, y : y + 8, :] for x in range(SLAB)]
                )
            if o > 0:
                along_z(0, s, o - 1)
        along_z(0, s, orbs - 1)

        send_slab(0, s)

        @pl.loop(0, SLAB)
        def _(x):
            q[x0 + x] = 24.0 * q[x0 + x] - 18.0

    for level in range(3):
        src, dst = level % 2, (level + 1) % 2

        @pl.loop(0, slabs)
        def _(i, level=level, src=src, dst=dst):
            s = lax.rem(i + 1, slabs)
            x0 = s * SLAB
            for side in range(2):

                @pl.when(receives(1, side))
                def _():
                    y_copy(level, side, s).wait_recv()

                @pl.when(receives(2, side))
                def _():
                    z_copy(level, side, s).wait_recv()

                @pl.when(
                    jnp.logical_and(
                        receives(0, side), s == (0 if side == 0 else slabs - 1)
                    )
                )
                def _():
                    x_copy(level, side).wait_recv()

                if level == 1:

                    @pl.when(sends(1, side))
                    def _():
                        y_copy(0, side, s).wait_send()

            def advance(o):
                for g in range(groups):
                    delta = (
                        jnp.where(phase < 2, zin[level, 0, s, o, g], zin[level, 1, s, o, g])
                        - own[level, s, o, g]
                    )
                    far = jnp.where(
                        phase < 2,
                        pltpu.roll(delta, LANES - 2, 1),
                        pltpu.roll(delta, 2, 1),
                    )
                    near = jnp.where(
                        phase == 1,
                        pltpu.roll(delta, LANES - 1, 1),
                        jnp.where(phase == 2, pltpu.roll(delta, 1, 1), 0.0),
                    )
                    fix = far - 16.0 * near
                    for b in range(4):
                        y = ROW0 + 8 * (4 * g + b)
                        c = [u[src, o, x0 + j, y : y + 8, :] for j in range(SLAB + 4)]
                        news = []
                        for x in range(SLAB):
                            k = b * SLAB + x
                            v = c[x + 2]
                            px = x0 + 2 + x

                            def row(d):
                                return u[src, o, px, y + d : y + d + 8, :]

                            one = (c[x + 1] + c[x + 3]) + (row(-1) + row(1))
                            two = (c[x] + c[x + 4]) + (row(-2) + row(2))
                            cor = jnp.where(
                                edge, pltpu.roll(fix, (2 * LANES - 4 * k - 2) % LANES, 1), 0.0
                            )
                            total = (
                                q[x0 + x, y - ROW0 : y - ROW0 + 8, :] * v
                                + (zp[o, x0 + x, y - ROW0 : y - ROW0 + 8, :] + cor)
                                + two
                                - 16.0 * one
                            )
                            if level == 0:
                                new = total * (1.0 / 84.0)
                            else:
                                new = total * (1.0 / 42.0) - u[dst, o, px, y : y + 8, :]
                            if level < 2:
                                u[dst, o, px, y : y + 8, :] = new
                                news.append(new)
                            else:
                                out[o, x0 + x, y - ROW0 : y - ROW0 + 8, :] = new
                        if level < 2:
                            row = SLAB * (y - ROW0)
                            half[o, row : row + 8 * SLAB, :] = halves(news)

            if level < 2:
                for o in range(orbs):
                    advance(o)
                    if o > 0:
                        along_z(level + 1, s, o - 1)
                along_z(level + 1, s, orbs - 1)
            else:
                pl.loop(0, orbs)(advance)

            if level < 2:
                send_slab(level + 1, s)
                for side in range(2):

                    @pl.when(
                        jnp.logical_and(sends(0, side), s == (slabs - 1 if side == 0 else 0))
                    )
                    def _():
                        x_copy(level + 1, side).start()

            else:

                @pl.when(i == 0)
                def _():
                    acc[...] = jnp.zeros_like(acc)

                @pl.loop(0, SLAB)
                def _(x):
                    sums = [None] * 10
                    for b in range(blocks):
                        f = [out[o, x0 + x, 8 * b : 8 * b + 8, :] for o in range(orbs)]
                        n = 0
                        for o in range(orbs):
                            for p in range(o, orbs):
                                term = f[o] * f[p]
                                sums[n] = term if sums[n] is None else sums[n] + term
                                n += 1
                    for n in range(10):
                        acc[n] = acc[n] + sums[n]

    total = jnp.concatenate(
        [jnp.sum(acc[n], axis=0, keepdims=True) for n in range(10)]
        + [jnp.zeros((6, LANES), jnp.float32)],
        axis=0,
    )
    for axis, slots, ss, rs in ((2, g0, g0s, g0r), (1, g1, g1s, g1r), (0, g2, g2s, g2r)):
        me, count = here[axis], counts[axis]
        slots[me] = total

        def g_copy(k):
            return pltpu.make_async_remote_copy(
                src_ref=slots.at[me],
                dst_ref=slots.at[me],
                send_sem=ss.at[k],
                recv_sem=rs.at[k],
                device_id=device(axis, lax.rem(me + k, count)),
                device_id_type=MESH,
            )

        def g_arrival(k):
            peer = lax.rem(me + count - k, count)
            return pltpu.make_async_remote_copy(
                src_ref=slots.at[peer],
                dst_ref=slots.at[peer],
                send_sem=ss.at[k],
                recv_sem=rs.at[k],
                device_id=device(axis, peer),
                device_id_type=MESH,
            )

        for k in range(1, count):
            g_copy(k).start()
        for k in range(1, count):
            g_arrival(k).wait_recv()
        total = slots[0]
        for k in range(1, count):
            total = total + slots[k]
        for k in range(1, count):
            g_copy(k).wait_send()
    gram[...] = total

    for level in range(3):
        for side in range(2):

            @pl.when(sends(0, side))
            def _():
                x_copy(level, side).wait_send()

            @pl.loop(0, slabs)
            def _(s):
                if level > 0:

                    @pl.when(sends(1, side))
                    def _():
                        y_copy(level, side, s).wait_send()

                @pl.when(sends(2, side))
                def _():
                    z_copy(level, side, s).wait_send()


def basis_kernel(cells, filtered, gram, basis, factor, inv):
    @pl.when(pl.program_id(0) == 0)
    def _():
        sums = jnp.sum(gram[...], axis=1, keepdims=True) * (1.0 / cells)
        sums = jnp.broadcast_to(sums, (16, LANES))
        g, n = {}, 0
        for i in range(4):
            for j in range(i, 4):
                g[i, j] = sums[n : n + 1, :]
                n += 1
        r = {}
        for i in range(4):
            for j in range(i, 4):
                value = g[i, j]
                for m in range(i):
                    value = value - r[m, i] * r[m, j]
                r[i, j] = jnp.sqrt(value) if i == j else value / r[i, i]
        w = {}
        for j in range(4):
            w[j, j] = 1.0 / r[j, j]
            for i in range(j - 1, -1, -1):
                value = r[i, i + 1] * w[i + 1, j]
                for m in range(i + 2, j + 1):
                    value = value + r[i, m] * w[m, j]
                w[i, j] = -value / r[i, i]
        n = 0
        for i in range(4):
            for j in range(i, 4):
                inv[n] = jnp.broadcast_to(w[i, j], (8, LANES))
                n += 1
        line = lax.broadcasted_iota(jnp.int32, (4, 4), 0)
        column = lax.broadcasted_iota(jnp.int32, (4, 4), 1)
        table = jnp.zeros((4, 4), jnp.float32)
        for i in range(4):
            for j in range(i, 4):
                table = jnp.where(
                    (line == i) & (column == j), jnp.broadcast_to(r[i, j][:, :4], (4, 4)), table
                )
        factor[...] = table

    w, n = {}, 0
    for i in range(4):
        for j in range(i, 4):
            w[i, j] = inv[n]
            n += 1
    planes, ny = basis.shape[1], basis.shape[2]
    x0 = pl.program_id(0) * planes

    @pl.loop(0, planes)
    def _(x):
        for b in range(ny // 8):
            f = [filtered[o, x0 + x, 8 * b : 8 * b + 8, :] for o in range(4)]
            for j in range(4):
                value = f[0] * w[0, j]
                for i in range(1, j + 1):
                    value = value + f[i] * w[i, j]
                basis[j, x, 8 * b : 8 * b + 8, :] = value


def body(orbitals, potential):
    orbs, nx, ny, nz = orbitals.shape
    cx, cy, cz = (lax.axis_size(a) for a in ("gx", "gy", "gz"))
    slabs, groups = nx // SLAB, ny // 32
    dma = pltpu.SemaphoreType.DMA
    f32 = jnp.float32
    filtered, gram = pl.pallas_call(
        functools.partial(filter_kernel, (nx, ny, cx, cy, cz)),
        out_shape=(
            pltpu.VMEM(orbitals.shape, f32),
            pltpu.VMEM((16, LANES), f32),
        ),
        in_specs=[pl.BlockSpec(memory_space=pl.ANY)] * 2,
        out_specs=(
            pl.BlockSpec(memory_space=pltpu.VMEM),
            pl.BlockSpec(memory_space=pltpu.VMEM),
        ),
        scratch_shapes=[
            pltpu.VMEM((2, orbs, nx + 4, ny + 16, nz), f32),
            pltpu.VMEM((nx, ny, nz), f32),
            pltpu.VMEM((orbs, nx, ny, nz), f32),
            pltpu.VMEM((orbs, SLAB * ny, 2 * nz), jnp.bfloat16),
            pltpu.VMEM((2 * nz, 2 * nz), jnp.bfloat16),
            pltpu.VMEM((3, slabs, orbs, groups, 8, LANES), f32),
            pltpu.VMEM((3, 2, slabs, orbs, groups, 8, LANES), f32),
            pltpu.VMEM((10, 8, LANES), f32),
            pltpu.VMEM((cz, 16, LANES), f32),
            pltpu.VMEM((cy, 16, LANES), f32),
            pltpu.VMEM((cx, 16, LANES), f32),
            dma((slabs,)),
            dma((slabs,)),
            dma((3, 2)),
            dma((3, 2)),
            dma((3, 2, slabs)),
            dma((3, 2, slabs)),
            dma((3, 2, slabs)),
            dma((3, 2, slabs)),
            dma((cz,)),
            dma((cz,)),
            dma((cy,)),
            dma((cy,)),
            dma((cx,)),
            dma((cx,)),
        ],
        compiler_params=pltpu.CompilerParams(
            collective_id=0, has_side_effects=True, vmem_limit_bytes=48 << 20
        ),
    )(orbitals, potential)
    planes = 8
    basis, factor = pl.pallas_call(
        functools.partial(basis_kernel, nx * cx * ny * cy * nz * cz),
        grid=(nx // planes,),
        out_shape=(
            jax.ShapeDtypeStruct(orbitals.shape, f32),
            jax.ShapeDtypeStruct((4, 4), f32),
        ),
        in_specs=[
            pl.BlockSpec(memory_space=pltpu.VMEM),
            pl.BlockSpec(memory_space=pltpu.VMEM),
        ],
        out_specs=(
            pl.BlockSpec((orbs, planes, ny, nz), lambda i: (0, i, 0, 0)),
            pl.BlockSpec((4, 4), lambda i: (0, 0)),
        ),
        scratch_shapes=[pltpu.VMEM((10, 8, LANES), f32)],
        compiler_params=pltpu.CompilerParams(vmem_limit_bytes=24 << 20),
    )(
        pltpu.with_memory_space_constraint(filtered, pltpu.VMEM),
        pltpu.with_memory_space_constraint(gram, pltpu.VMEM),
    )
    return basis, factor


def solution(mesh):
    return jax.shard_map(
        body,
        mesh=mesh,
        in_specs=(P(None, "gx", "gy", "gz"), P("gx", "gy", "gz")),
        out_specs=(P(None, "gx", "gy", "gz"), P()),
        check_vma=False,
    )
```

```python
import functools

import jax
import jax.numpy as jnp
from jax import lax
from jax.experimental import pallas as pl
from jax.experimental.pallas import tpu as pltpu
from jax.sharding import PartitionSpec as P

MESH = pl.DeviceIdType.MESH
LANES = 128
SLAB = 8
ROW0 = 8


def merge(tree, value, lane):
    size = 0
    while tree and tree[-1][0] == size:
        low = tree.pop()[1]
        value = jnp.where((lane & (4 << size)) != 0, value, low)
        size += 1
    tree.append((size, value))


def halves(rows):
    parts = []
    for k in range(0, len(rows), 2):
        pair = jnp.concatenate(rows[k : k + 2], axis=0)
        high = pair.astype(jnp.bfloat16)
        low = (pair - high.astype(jnp.float32)).astype(jnp.bfloat16)
        parts.append(jnp.concatenate([high, low], axis=1))
    return jnp.concatenate(parts, axis=0)


def filter_kernel(
    sizes, orb, pot, out, gram, u, q, zp, half, weights, own, zin, acc, g0, g1,
    load_sem, pot_sem, xs, xr, ys, yr, zs, zr, g0s, g0r, g1s, g1r,
):
    nx, ny, cx, cy, cz = sizes
    slabs = nx // SLAB
    blocks = ny // 8
    groups = blocks // 4
    orbs = 4
    gx, gy, gz = lax.axis_index("gx"), lax.axis_index("gy"), lax.axis_index("gz")
    here = [gx, gy, gz]
    counts = [cx, cy, cz]

    def device(axis, index):
        return tuple(index if a == axis else here[a] for a in range(3))

    def load(s):
        x0 = s * SLAB
        return (
            pltpu.make_async_copy(
                orb.at[:, pl.ds(x0, SLAB)],
                u.at[0, :, pl.ds(2 + x0, SLAB), pl.ds(ROW0, ny)],
                load_sem.at[s],
            ),
            pltpu.make_async_copy(
                pot.at[pl.ds(x0, SLAB)], q.at[pl.ds(x0, SLAB)], pot_sem.at[s]
            ),
        )

    @pl.loop(0, slabs)
    def _(i):
        for copy in load(lax.rem(i + 1, slabs)):
            copy.start()

    plane = cx * cy
    spot = gx * cy + gy

    def line_peer(k):
        return (gx, gy, lax.rem(gz + k, cz))

    def plane_peer(k):
        peer = lax.rem(spot + k, plane)
        return (lax.div(peer, cy), lax.rem(peer, cy), gz)

    barrier = pltpu.get_barrier_semaphore()
    for count, peer in ((cz, line_peer), (plane, plane_peer)):
        for k in range(1, count):
            pl.semaphore_signal(
                barrier, inc=1, device_id=peer(k), device_id_type=MESH
            )

    def x_copy(level, side):
        buf = level % 2
        first = nx if side == 0 else 2
        target = 0 if side == 0 else nx + 2
        if level == 0:
            source = orb.at[:, pl.ds(first - 2, 2)]
        else:
            source = u.at[buf, :, pl.ds(first, 2), pl.ds(ROW0, ny)]
        return pltpu.make_async_remote_copy(
            src_ref=source,
            dst_ref=u.at[buf, :, pl.ds(target, 2), pl.ds(ROW0, ny)],
            send_sem=xs.at[level, side],
            recv_sem=xr.at[level, side],
            device_id=device(0, gx + 1 if side == 0 else gx - 1),
            device_id_type=MESH,
        )

    def y_copy(level, side, s):
        buf = level % 2
        planes = pl.ds(2 + s * SLAB, SLAB)
        first = ROW0 + ny - 2 if side == 0 else ROW0
        target = ROW0 - 2 if side == 0 else ROW0 + ny
        return pltpu.make_async_remote_copy(
            src_ref=u.at[buf, :, planes, pl.ds(first, 2)],
            dst_ref=u.at[buf, :, planes, pl.ds(target, 2)],
            send_sem=ys.at[level, side, s],
            recv_sem=yr.at[level, side, s],
            device_id=device(1, gy + 1 if side == 0 else gy - 1),
            device_id_type=MESH,
        )

    def z_copy(level, side, s):
        return pltpu.make_async_remote_copy(
            src_ref=own.at[level, s],
            dst_ref=zin.at[level, side, s],
            send_sem=zs.at[level, side, s],
            recv_sem=zr.at[level, side, s],
            device_id=device(2, gz + 1 if side == 0 else gz - 1),
            device_id_type=MESH,
        )

    def sends(axis, side):
        return here[axis] < counts[axis] - 1 if side == 0 else here[axis] > 0

    def receives(axis, side):
        return here[axis] > 0 if side == 0 else here[axis] < counts[axis] - 1

    def send_slab(level, s):
        for side in range(2):

            @pl.when(sends(1, side))
            def _():
                y_copy(level, side, s).start()

            @pl.when(sends(2, side))
            def _():
                z_copy(level, side, s).start()

    for side in range(2):
        xt = 0 if side == 0 else nx + 2
        yt = ROW0 - 2 if side == 0 else ROW0 + ny

        @pl.when(jnp.logical_not(receives(0, side)))
        def _():
            @pl.loop(0, orbs)
            def _(o):
                for buf in range(2):
                    for plane in range(2):
                        u[buf, o, xt + plane, ROW0 : ROW0 + ny, :] = jnp.zeros(
                            (ny, LANES), jnp.float32
                        )

        @pl.when(jnp.logical_not(receives(1, side)))
        def _():
            @pl.loop(0, orbs)
            def _(o):
                @pl.loop(0, slabs)
                def _(s):
                    for x in range(SLAB):
                        for buf in range(2):
                            u[buf, o, 2 + s * SLAB + x, yt : yt + 2, :] = jnp.zeros(
                                (2, LANES), jnp.float32
                            )

        @pl.when(jnp.logical_not(receives(2, side)))
        def _():
            @pl.loop(0, slabs)
            def _(s):
                for level in range(3):
                    zin[level, side, s] = jnp.zeros((orbs, groups, 8, LANES), jnp.float32)

    lane = lax.broadcasted_iota(jnp.int32, (8, LANES), 1)
    phase = lane & 3
    edge = (lane < 2) | (lane >= LANES - 2)

    source = lax.broadcasted_iota(jnp.int32, (2 * LANES, 2 * LANES), 0) & (LANES - 1)
    target = lax.broadcasted_iota(jnp.int32, (2 * LANES, 2 * LANES), 1)
    step = (target - source) & (LANES - 1)
    band = jnp.where(
        (step == 1) | (step == LANES - 1),
        -16.0,
        jnp.where((step == 2) | (step == LANES - 2), 1.0, 0.0),
    )
    ends = jnp.where((target & 3) == ((source + 2) & (LANES - 1)), 1.0, 0.0)
    weights[...] = jnp.where(target < LANES, band, ends).astype(jnp.bfloat16)

    pl.semaphore_wait(barrier, cz + plane - 2)
    for side in range(2):

        @pl.when(sends(0, side))
        def _():
            x_copy(0, side).start()

    def along_z(level, s, o):
        done = jnp.dot(half[o], weights[...], preferred_element_type=jnp.float32)
        for g in range(groups):
            tree = []
            for b in range(4 * g, 4 * g + 4):
                for x in range(SLAB):
                    row = 8 * (b * SLAB + x)
                    zp[o, s * SLAB + x, 8 * b : 8 * b + 8, :] = done[row : row + 8, :LANES]
                    merge(tree, done[row : row + 8, LANES:], lane)
            own[level, s, o, g] = tree[0][1]

    @pl.loop(0, slabs)
    def _(i):
        s = lax.rem(i + 1, slabs)
        x0 = s * SLAB
        for copy in load(s):
            copy.wait()

        for o in range(orbs):
            for b in range(blocks):
                y = ROW0 + 8 * b
                half[o, SLAB * 8 * b : SLAB * 8 * (b + 1), :] = halves(
                    [u[0, o, x0 + 2 + x, y : y + 8, :] for x in range(SLAB)]
                )
            if o > 0:
                along_z(0, s, o - 1)
        along_z(0, s, orbs - 1)

        send_slab(0, s)

        @pl.loop(0, SLAB)
        def _(x):
            q[x0 + x] = 24.0 * q[x0 + x] - 18.0

    for level in range(3):
        src, dst = level % 2, (level + 1) % 2

        @pl.loop(0, slabs)
        def _(i, level=level, src=src, dst=dst):
            s = lax.rem(i + 1, slabs)
            x0 = s * SLAB
            for side in range(2):

                @pl.when(receives(1, side))
                def _():
                    y_copy(level, side, s).wait_recv()

                @pl.when(receives(2, side))
                def _():
                    z_copy(level, side, s).wait_recv()

                @pl.when(
                    jnp.logical_and(
                        receives(0, side), s == (0 if side == 0 else slabs - 1)
                    )
                )
                def _():
                    x_copy(level, side).wait_recv()

                if level == 1:

                    @pl.when(sends(1, side))
                    def _():
                        y_copy(0, side, s).wait_send()

            def advance(o):
                for g in range(groups):
                    delta = (
                        jnp.where(phase < 2, zin[level, 0, s, o, g], zin[level, 1, s, o, g])
                        - own[level, s, o, g]
                    )
                    far = jnp.where(
                        phase < 2,
                        pltpu.roll(delta, LANES - 2, 1),
                        pltpu.roll(delta, 2, 1),
                    )
                    near = jnp.where(
                        phase == 1,
                        pltpu.roll(delta, LANES - 1, 1),
                        jnp.where(phase == 2, pltpu.roll(delta, 1, 1), 0.0),
                    )
                    fix = far - 16.0 * near
                    for b in range(4):
                        y = ROW0 + 8 * (4 * g + b)
                        c = [u[src, o, x0 + j, y : y + 8, :] for j in range(SLAB + 4)]
                        news = []
                        for x in range(SLAB):
                            k = b * SLAB + x
                            v = c[x + 2]
                            px = x0 + 2 + x

                            def row(d):
                                return u[src, o, px, y + d : y + d + 8, :]

                            one = (c[x + 1] + c[x + 3]) + (row(-1) + row(1))
                            two = (c[x] + c[x + 4]) + (row(-2) + row(2))
                            cor = jnp.where(
                                edge, pltpu.roll(fix, (2 * LANES - 4 * k - 2) % LANES, 1), 0.0
                            )
                            total = (
                                q[x0 + x, y - ROW0 : y - ROW0 + 8, :] * v
                                + (zp[o, x0 + x, y - ROW0 : y - ROW0 + 8, :] + cor)
                                + two
                                - 16.0 * one
                            )
                            if level == 0:
                                new = total * (1.0 / 84.0)
                            else:
                                new = total * (1.0 / 42.0) - u[dst, o, px, y : y + 8, :]
                            if level < 2:
                                u[dst, o, px, y : y + 8, :] = new
                                news.append(new)
                            else:
                                out[o, x0 + x, y - ROW0 : y - ROW0 + 8, :] = new
                        if level < 2:
                            row = SLAB * (y - ROW0)
                            half[o, row : row + 8 * SLAB, :] = halves(news)

            if level < 2:
                for o in range(orbs):
                    advance(o)
                    if o > 0:
                        along_z(level + 1, s, o - 1)
                along_z(level + 1, s, orbs - 1)
            else:
                pl.loop(0, orbs)(advance)

            if level < 2:
                send_slab(level + 1, s)
                for side in range(2):

                    @pl.when(
                        jnp.logical_and(sends(0, side), s == (slabs - 1 if side == 0 else 0))
                    )
                    def _():
                        x_copy(level + 1, side).start()

            else:

                @pl.when(i == 0)
                def _():
                    acc[...] = jnp.zeros_like(acc)

                @pl.loop(0, SLAB)
                def _(x):
                    sums = [None] * 10
                    for b in range(blocks):
                        f = [out[o, x0 + x, 8 * b : 8 * b + 8, :] for o in range(orbs)]
                        n = 0
                        for o in range(orbs):
                            for p in range(o, orbs):
                                term = f[o] * f[p]
                                sums[n] = term if sums[n] is None else sums[n] + term
                                n += 1
                    for n in range(10):
                        acc[n] = acc[n] + sums[n]

    rows = [jnp.sum(acc[n], axis=0, keepdims=True) for n in range(10)]
    first = jnp.concatenate(rows[:8], axis=0)
    second = jnp.concatenate(rows[8:] + [jnp.zeros((6, LANES), jnp.float32)], axis=0)
    half_lanes = LANES // 2
    total = jnp.where(
        lane < half_lanes,
        first + pltpu.roll(first, half_lanes, 1),
        second + pltpu.roll(second, half_lanes, 1),
    )
    stages = (
        (gz, cz, line_peer, g0, g0s, g0r),
        (spot, plane, plane_peer, g1, g1s, g1r),
    )

    def sum_copy(stage, k, arrival):
        me, count, peer, slots, ss, rs = stage
        slot = slots.at[lax.rem(me + count - k, count) if arrival else me]
        return pltpu.make_async_remote_copy(
            src_ref=slot,
            dst_ref=slot,
            send_sem=ss.at[k],
            recv_sem=rs.at[k],
            device_id=peer(k),
            device_id_type=MESH,
        )

    for stage in stages:
        me, count, _, slots, _, _ = stage
        slots[me] = total
        for k in range(1, count):
            sum_copy(stage, k, False).start()
        for k in range(1, count):
            sum_copy(stage, k, True).wait_recv()
        total = slots[0]
        for k in range(1, count):
            total = total + slots[k]
    gram[...] = total
    for stage in stages:
        for k in range(1, stage[1]):
            sum_copy(stage, k, False).wait_send()

    for level in range(3):
        for side in range(2):

            @pl.when(sends(0, side))
            def _():
                x_copy(level, side).wait_send()

            @pl.loop(0, slabs)
            def _(s):
                if level > 0:

                    @pl.when(sends(1, side))
                    def _():
                        y_copy(level, side, s).wait_send()

                @pl.when(sends(2, side))
                def _():
                    z_copy(level, side, s).wait_send()


def basis_kernel(cells, filtered, gram, basis, factor, inv):
    @pl.when(pl.program_id(0) == 0)
    def _():
        lower = lax.broadcasted_iota(jnp.int32, (8, LANES), 1) < LANES // 2
        sums = [
            jnp.broadcast_to(
                jnp.sum(jnp.where(part, gram[...], 0.0), axis=1, keepdims=True) * (1.0 / cells),
                (8, LANES),
            )
            for part in (lower, jnp.logical_not(lower))
        ]
        g, n = {}, 0
        for i in range(4):
            for j in range(i, 4):
                g[i, j] = sums[n // 8][n % 8 : n % 8 + 1, :]
                n += 1
        r = {}
        for i in range(4):
            for j in range(i, 4):
                value = g[i, j]
                for m in range(i):
                    value = value - r[m, i] * r[m, j]
                r[i, j] = jnp.sqrt(value) if i == j else value / r[i, i]
        w = {}
        for j in range(4):
            w[j, j] = 1.0 / r[j, j]
            for i in range(j - 1, -1, -1):
                value = r[i, i + 1] * w[i + 1, j]
                for m in range(i + 2, j + 1):
                    value = value + r[i, m] * w[m, j]
                w[i, j] = -value / r[i, i]
        n = 0
        for i in range(4):
            for j in range(i, 4):
                inv[n] = jnp.broadcast_to(w[i, j], (8, LANES))
                n += 1
        line = lax.broadcasted_iota(jnp.int32, (4, 4), 0)
        column = lax.broadcasted_iota(jnp.int32, (4, 4), 1)
        table = jnp.zeros((4, 4), jnp.float32)
        for i in range(4):
            for j in range(i, 4):
                table = jnp.where(
                    (line == i) & (column == j), jnp.broadcast_to(r[i, j][:, :4], (4, 4)), table
                )
        factor[...] = table

    w, n = {}, 0
    for i in range(4):
        for j in range(i, 4):
            w[i, j] = inv[n]
            n += 1
    planes, ny = basis.shape[1], basis.shape[2]
    x0 = pl.program_id(0) * planes

    @pl.loop(0, planes)
    def _(x):
        for b in range(ny // 8):
            f = [filtered[o, x0 + x, 8 * b : 8 * b + 8, :] for o in range(4)]
            for j in range(4):
                value = f[0] * w[0, j]
                for i in range(1, j + 1):
                    value = value + f[i] * w[i, j]
                basis[j, x, 8 * b : 8 * b + 8, :] = value


def body(orbitals, potential):
    orbs, nx, ny, nz = orbitals.shape
    cx, cy, cz = (lax.axis_size(a) for a in ("gx", "gy", "gz"))
    slabs, groups = nx // SLAB, ny // 32
    dma = pltpu.SemaphoreType.DMA
    f32 = jnp.float32
    filtered, gram = pl.pallas_call(
        functools.partial(filter_kernel, (nx, ny, cx, cy, cz)),
        out_shape=(
            pltpu.VMEM(orbitals.shape, f32),
            pltpu.VMEM((8, LANES), f32),
        ),
        in_specs=[pl.BlockSpec(memory_space=pl.ANY)] * 2,
        out_specs=(
            pl.BlockSpec(memory_space=pltpu.VMEM),
            pl.BlockSpec(memory_space=pltpu.VMEM),
        ),
        scratch_shapes=[
            pltpu.VMEM((2, orbs, nx + 4, ny + 16, nz), f32),
            pltpu.VMEM((nx, ny, nz), f32),
            pltpu.VMEM((orbs, nx, ny, nz), f32),
            pltpu.VMEM((orbs, SLAB * ny, 2 * nz), jnp.bfloat16),
            pltpu.VMEM((2 * nz, 2 * nz), jnp.bfloat16),
            pltpu.VMEM((3, slabs, orbs, groups, 8, LANES), f32),
            pltpu.VMEM((3, 2, slabs, orbs, groups, 8, LANES), f32),
            pltpu.VMEM((10, 8, LANES), f32),
            pltpu.VMEM((cz, 8, LANES), f32),
            pltpu.VMEM((cx * cy, 8, LANES), f32),
            dma((slabs,)),
            dma((slabs,)),
            dma((3, 2)),
            dma((3, 2)),
            dma((3, 2, slabs)),
            dma((3, 2, slabs)),
            dma((3, 2, slabs)),
            dma((3, 2, slabs)),
            dma((cz,)),
            dma((cz,)),
            dma((cx * cy,)),
            dma((cx * cy,)),
        ],
        compiler_params=pltpu.CompilerParams(
            collective_id=0, has_side_effects=True, vmem_limit_bytes=48 << 20
        ),
    )(orbitals, potential)
    planes = 8
    basis, factor = pl.pallas_call(
        functools.partial(basis_kernel, nx * cx * ny * cy * nz * cz),
        grid=(nx // planes,),
        out_shape=(
            jax.ShapeDtypeStruct(orbitals.shape, f32),
            jax.ShapeDtypeStruct((4, 4), f32),
        ),
        in_specs=[
            pl.BlockSpec(memory_space=pltpu.VMEM),
            pl.BlockSpec(memory_space=pltpu.VMEM),
        ],
        out_specs=(
            pl.BlockSpec((orbs, planes, ny, nz), lambda i: (0, i, 0, 0)),
            pl.BlockSpec((4, 4), lambda i: (0, 0)),
        ),
        scratch_shapes=[pltpu.VMEM((10, 8, LANES), f32)],
        compiler_params=pltpu.CompilerParams(vmem_limit_bytes=24 << 20),
    )(
        pltpu.with_memory_space_constraint(filtered, pltpu.VMEM),
        pltpu.with_memory_space_constraint(gram, pltpu.VMEM),
    )
    return basis, factor


def solution(mesh):
    return jax.shard_map(
        body,
        mesh=mesh,
        in_specs=(P(None, "gx", "gy", "gz"), P("gx", "gy", "gz")),
        out_specs=(P(None, "gx", "gy", "gz"), P()),
        check_vma=False,
    )
```

```python
import functools

import jax
import jax.numpy as jnp
from jax import lax
from jax.experimental import pallas as pl
from jax.experimental.pallas import tpu as pltpu
from jax.sharding import PartitionSpec as P

MESH = pl.DeviceIdType.MESH
LANES = 128
SLAB = 8
ROW0 = 8


def merge(tree, value, lane):
    size = 0
    while tree and tree[-1][0] == size:
        low = tree.pop()[1]
        value = jnp.where((lane & (4 << size)) != 0, value, low)
        size += 1
    tree.append((size, value))


def halves(rows):
    parts = []
    for k in range(0, len(rows), 2):
        pair = jnp.concatenate(rows[k : k + 2], axis=0)
        high = pair.astype(jnp.bfloat16)
        low = (pair - high.astype(jnp.float32)).astype(jnp.bfloat16)
        parts.append(jnp.concatenate([high, low], axis=1))
    return jnp.concatenate(parts, axis=0)


def filter_kernel(
    sizes, orb, pot, out, gram, u, q, zp, zl, half, weights, own, zin, acc, g0, g1,
    load_sem, pot_sem, xs, xr, ys, yr, zs, zr, g0s, g0r, g1s, g1r,
):
    nx, ny, cx, cy, cz = sizes
    slabs = nx // SLAB
    blocks = ny // 8
    groups = blocks // 4
    orbs = 4
    gx, gy, gz = lax.axis_index("gx"), lax.axis_index("gy"), lax.axis_index("gz")
    here = [gx, gy, gz]
    counts = [cx, cy, cz]

    def device(axis, index):
        return tuple(index if a == axis else here[a] for a in range(3))

    def load(s):
        x0 = s * SLAB
        return (
            pltpu.make_async_copy(
                orb.at[:, pl.ds(x0, SLAB)],
                u.at[0, :, pl.ds(2 + x0, SLAB), pl.ds(ROW0, ny)],
                load_sem.at[s],
            ),
            pltpu.make_async_copy(
                pot.at[pl.ds(x0, SLAB)], q.at[pl.ds(x0, SLAB)], pot_sem.at[s]
            ),
        )

    @pl.loop(0, slabs)
    def _(i):
        for copy in load(lax.rem(i + 1, slabs)):
            copy.start()

    plane = cx * cy
    spot = gx * cy + gy
    far = lambda k, count: -min(k, count - k)
    line = sorted(range(1, cz), key=lambda k: far(k, cz))
    square = sorted(range(1, plane), key=lambda k: far(k // cy, cx) + far(k % cy, cy))

    def line_peer(k, sign):
        return (gx, gy, lax.rem(gz + cz + sign * k, cz))

    def plane_peer(k, sign):
        dx, dy = sign * (k // cy), sign * (k % cy)
        return (lax.rem(gx + cx + dx, cx), lax.rem(gy + cy + dy, cy), gz)

    barrier = pltpu.get_barrier_semaphore()
    for order, peer in ((line, line_peer), (square, plane_peer)):
        for k in order:
            pl.semaphore_signal(
                barrier, inc=1, device_id=peer(k, 1), device_id_type=MESH
            )

    def x_copy(level, side):
        buf = level % 2
        first = nx if side == 0 else 2
        target = 0 if side == 0 else nx + 2
        if level == 0:
            source = orb.at[:, pl.ds(first - 2, 2)]
        else:
            source = u.at[buf, :, pl.ds(first, 2), pl.ds(ROW0, ny)]
        return pltpu.make_async_remote_copy(
            src_ref=source,
            dst_ref=u.at[buf, :, pl.ds(target, 2), pl.ds(ROW0, ny)],
            send_sem=xs.at[level, side],
            recv_sem=xr.at[level, side],
            device_id=device(0, gx + 1 if side == 0 else gx - 1),
            device_id_type=MESH,
        )

    def y_copy(level, side, s):
        buf = level % 2
        planes = pl.ds(2 + s * SLAB, SLAB)
        first = ROW0 + ny - 2 if side == 0 else ROW0
        target = ROW0 - 2 if side == 0 else ROW0 + ny
        return pltpu.make_async_remote_copy(
            src_ref=u.at[buf, :, planes, pl.ds(first, 2)],
            dst_ref=u.at[buf, :, planes, pl.ds(target, 2)],
            send_sem=ys.at[level, side, s],
            recv_sem=yr.at[level, side, s],
            device_id=device(1, gy + 1 if side == 0 else gy - 1),
            device_id_type=MESH,
        )

    def z_copy(level, side, s):
        return pltpu.make_async_remote_copy(
            src_ref=own.at[level, s],
            dst_ref=zin.at[level, side, s],
            send_sem=zs.at[level, side, s],
            recv_sem=zr.at[level, side, s],
            device_id=device(2, gz + 1 if side == 0 else gz - 1),
            device_id_type=MESH,
        )

    def sends(axis, side):
        return here[axis] < counts[axis] - 1 if side == 0 else here[axis] > 0

    def receives(axis, side):
        return here[axis] > 0 if side == 0 else here[axis] < counts[axis] - 1

    def send_rows(level, s):
        for side in range(2):

            @pl.when(sends(1, side))
            def _():
                y_copy(level, side, s).start()

    def send_ends(level, s):
        for side in range(2):

            @pl.when(sends(2, side))
            def _():
                z_copy(level, side, s).start()

    for side in range(2):
        xt = 0 if side == 0 else nx + 2
        yt = ROW0 - 2 if side == 0 else ROW0 + ny

        @pl.when(jnp.logical_not(receives(0, side)))
        def _():
            @pl.loop(0, orbs)
            def _(o):
                for buf in range(2):
                    for plane in range(2):
                        u[buf, o, xt + plane, ROW0 : ROW0 + ny, :] = jnp.zeros(
                            (ny, LANES), jnp.float32
                        )

        @pl.when(jnp.logical_not(receives(1, side)))
        def _():
            @pl.loop(0, orbs)
            def _(o):
                @pl.loop(0, slabs)
                def _(s):
                    for x in range(SLAB):
                        for buf in range(2):
                            u[buf, o, 2 + s * SLAB + x, yt : yt + 2, :] = jnp.zeros(
                                (2, LANES), jnp.float32
                            )

        @pl.when(jnp.logical_not(receives(2, side)))
        def _():
            @pl.loop(0, slabs)
            def _(s):
                for level in range(3):
                    zin[level, side, s] = jnp.zeros((orbs, groups, 8, LANES), jnp.float32)

    lane = lax.broadcasted_iota(jnp.int32, (8, LANES), 1)
    phase = lane & 3
    edge = (lane < 2) | (lane >= LANES - 2)

    source = lax.broadcasted_iota(jnp.int32, (2 * LANES, 2 * LANES), 0) & (LANES - 1)
    target = lax.broadcasted_iota(jnp.int32, (2 * LANES, 2 * LANES), 1)
    step = (target - source) & (LANES - 1)
    band = jnp.where(
        (step == 1) | (step == LANES - 1),
        -16.0,
        jnp.where((step == 2) | (step == LANES - 2), 1.0, 0.0),
    )
    ends = jnp.where((target & 3) == ((source + 2) & (LANES - 1)), 1.0, 0.0)
    weights[...] = jnp.where(target < LANES, band, ends).astype(jnp.bfloat16)

    pl.semaphore_wait(barrier, cz + plane - 2)
    for side in range(2):

        @pl.when(sends(0, side))
        def _():
            x_copy(0, side).start()

    pair = orbs // 2

    def along(o):
        return (zp, o) if o < pair else (zl, o - pair)

    def along_z(level, s, start, count):
        size = SLAB * ny
        done = jnp.dot(
            half[start : start + count].reshape(count * size, 2 * LANES),
            weights[...],
            preferred_element_type=jnp.float32,
        )
        for o in range(start, start + count):
            ref, part = along(o)
            for g in range(groups):
                tree = []
                for b in range(4 * g, 4 * g + 4):
                    for x in range(SLAB):
                        row = (o - start) * size + 8 * (b * SLAB + x)
                        ref[part, s * SLAB + x, 8 * b : 8 * b + 8, :] = done[
                            row : row + 8, :LANES
                        ]
                        merge(tree, done[row : row + 8, LANES:], lane)
                own[level, s, o, g] = tree[0][1]

    def enter(s, last):
        x0 = s * SLAB
        for copy in load(s):
            copy.wait()
        for o in range(orbs):
            for b in range(blocks):
                y = ROW0 + 8 * b
                half[o, SLAB * 8 * b : SLAB * 8 * (b + 1), :] = halves(
                    [u[0, o, x0 + 2 + x, y : y + 8, :] for x in range(SLAB)]
                )
        send_rows(0, s)
        along_z(0, s, 0, pair if last else orbs)
        if not last:
            send_ends(0, s)

        @pl.loop(0, SLAB)
        def _(x):
            q[x0 + x] = 24.0 * q[x0 + x] - 18.0

    @pl.loop(1, slabs)
    def _(s):
        enter(s, False)

    enter(0, True)

    def fixes(level, s, o, g):
        delta = (
            jnp.where(phase < 2, zin[level, 0, s, o, g], zin[level, 1, s, o, g])
            - own[level, s, o, g]
        )
        outer = jnp.where(
            phase < 2, pltpu.roll(delta, LANES - 2, 1), pltpu.roll(delta, 2, 1)
        )
        inner = jnp.where(
            phase == 1,
            pltpu.roll(delta, LANES - 1, 1),
            jnp.where(phase == 2, pltpu.roll(delta, 1, 1), 0.0),
        )
        return outer - 16.0 * inner

    def advance(level, s, o, fix):
        src, dst = level % 2, (level + 1) % 2
        x0 = s * SLAB
        ref, part = along(o)
        for b in range(blocks):
            y = ROW0 + 8 * b
            c = [u[src, o, x0 + j, y : y + 8, :] for j in range(SLAB + 4)]
            news = []
            for x in range(SLAB):
                k = (b % 4) * SLAB + x
                px = x0 + 2 + x

                def row(d):
                    return u[src, o, px, y + d : y + d + 8, :]

                one = (c[x + 1] + c[x + 3]) + (row(-1) + row(1))
                two = (c[x] + c[x + 4]) + (row(-2) + row(2))
                cor = jnp.where(
                    edge, pltpu.roll(fix[b // 4], (2 * LANES - 4 * k - 2) % LANES, 1), 0.0
                )
                total = (
                    q[x0 + x, 8 * b : 8 * b + 8, :] * c[x + 2]
                    + (ref[part, x0 + x, 8 * b : 8 * b + 8, :] + cor)
                    + two
                    - 16.0 * one
                )
                if level == 0:
                    new = total * (1.0 / 84.0)
                else:
                    new = total * (1.0 / 42.0) - u[dst, o, px, y : y + 8, :]
                if level < 2:
                    u[dst, o, px, y : y + 8, :] = new
                    news.append(new)
                else:
                    out[o, x0 + x, 8 * b : 8 * b + 8, :] = new
            if level < 2:
                row0 = SLAB * 8 * b
                half[o, row0 : row0 + 8 * SLAB, :] = halves(news)

    acc[...] = jnp.zeros_like(acc)

    for level in range(3):

        @pl.loop(0, slabs)
        def _(i, level=level):
            s = lax.rem(i + 1, slabs)
            x0 = s * SLAB
            for side in range(2):

                @pl.when(receives(1, side))
                def _():
                    y_copy(level, side, s).wait_recv()

                @pl.when(receives(2, side))
                def _():
                    z_copy(level, side, s).wait_recv()

                @pl.when(
                    jnp.logical_and(
                        receives(0, side), s == (0 if side == 0 else slabs - 1)
                    )
                )
                def _():
                    x_copy(level, side).wait_recv()

                if level == 1:

                    @pl.when(sends(1, side))
                    def _():
                        y_copy(0, side, s).wait_send()

            fix = [[fixes(level, s, o, g) for g in range(groups)] for o in range(orbs)]
            if level < 2:
                owner = level + lax.div(i + slabs - 1, slabs)
                along_z(owner, i, pair, pair)
            for o in range(orbs):
                advance(level, s, o, fix[o])
                if level < 2 and o == pair:
                    along_z(level + 1, s, 0, pair)
            if level < 2:
                send_rows(level + 1, s)
                send_ends(owner, i)
                for side in range(2):

                    @pl.when(
                        jnp.logical_and(sends(0, side), s == (slabs - 1 if side == 0 else 0))
                    )
                    def _():
                        x_copy(level + 1, side).start()

            else:
                sums = [None] * 10
                for x in range(SLAB):
                    for b in range(blocks):
                        f = [out[o, x0 + x, 8 * b : 8 * b + 8, :] for o in range(orbs)]
                        n = 0
                        for o in range(orbs):
                            for p in range(o, orbs):
                                term = f[o] * f[p]
                                sums[n] = term if sums[n] is None else sums[n] + term
                                n += 1
                for n in range(10):
                    acc[n] = acc[n] + sums[n]

        if level == 1:
            along_z(2, 0, pair, pair)
            send_ends(2, 0)

    rows = [jnp.sum(acc[n], axis=0, keepdims=True) for n in range(10)]
    first = jnp.concatenate(rows[:8], axis=0)
    second = jnp.concatenate(rows[8:] + [jnp.zeros((6, LANES), jnp.float32)], axis=0)
    half_lanes = LANES // 2
    total = jnp.where(
        lane < half_lanes,
        first + pltpu.roll(first, half_lanes, 1),
        second + pltpu.roll(second, half_lanes, 1),
    )
    stages = (
        (gz, cz, line, line_peer, lambda at: at[2], g0, g0s, g0r),
        (spot, plane, square, plane_peer, lambda at: at[0] * cy + at[1], g1, g1s, g1r),
    )

    def sum_copy(stage, k, arrival):
        me, _, _, peer, index, slots, ss, rs = stage
        slot = slots.at[index(peer(k, -1)) if arrival else me]
        return pltpu.make_async_remote_copy(
            src_ref=slot,
            dst_ref=slot,
            send_sem=ss.at[k],
            recv_sem=rs.at[k],
            device_id=peer(k, 1),
            device_id_type=MESH,
        )

    def sent():
        for level in range(3):
            for side in range(2):

                @pl.when(sends(0, side))
                def _():
                    x_copy(level, side).wait_send()

                @pl.loop(0, slabs)
                def _(s):
                    if level > 0:

                        @pl.when(sends(1, side))
                        def _():
                            y_copy(level, side, s).wait_send()

                    @pl.when(sends(2, side))
                    def _():
                        z_copy(level, side, s).wait_send()

    for stage in stages:
        me, count, order, slots = stage[0], stage[1], stage[2], stage[5]
        slots[me] = total
        for k in order:
            sum_copy(stage, k, False).start()
        if stage is stages[0]:
            sent()
        for k in reversed(order):
            sum_copy(stage, k, True).wait_recv()
        total = slots[0]
        for k in range(1, count):
            total = total + slots[k]
    gram[...] = total
    for stage in stages:
        for k in stage[2]:
            sum_copy(stage, k, False).wait_send()


def basis_kernel(cells, filtered, gram, basis, factor, stage, sem):
    def invert():
        lower = lax.broadcasted_iota(jnp.int32, (8, LANES), 1) < LANES // 2
        sums = [
            jnp.broadcast_to(
                jnp.sum(jnp.where(part, gram[...], 0.0), axis=1, keepdims=True) * (1.0 / cells),
                (8, LANES),
            )
            for part in (lower, jnp.logical_not(lower))
        ]
        g, n = {}, 0
        for i in range(4):
            for j in range(i, 4):
                g[i, j] = sums[n // 8][n % 8 : n % 8 + 1, :]
                n += 1
        r = {}
        for i in range(4):
            for j in range(i, 4):
                value = g[i, j]
                for m in range(i):
                    value = value - r[m, i] * r[m, j]
                r[i, j] = jnp.sqrt(value) if i == j else value / r[i, i]
        w = {}
        for j in range(4):
            w[j, j] = 1.0 / r[j, j]
            for i in range(j - 1, -1, -1):
                value = r[i, i + 1] * w[i + 1, j]
                for m in range(i + 2, j + 1):
                    value = value + r[i, m] * w[m, j]
                w[i, j] = -value / r[i, i]
        line = lax.broadcasted_iota(jnp.int32, (4, 4), 0)
        column = lax.broadcasted_iota(jnp.int32, (4, 4), 1)
        table = jnp.zeros((4, 4), jnp.float32)
        for i in range(4):
            for j in range(i, 4):
                table = jnp.where(
                    (line == i) & (column == j), jnp.broadcast_to(r[i, j][:, :4], (4, 4)), table
                )
        factor[...] = table
        return {at: jnp.broadcast_to(value, (8, LANES)) for at, value in w.items()}

    w = invert()
    nx, ny = basis.shape[1], basis.shape[2]
    chunks = sem.shape[0]
    planes = nx // chunks

    def write(c):
        part = pl.ds(c * planes, planes)
        return pltpu.make_async_copy(stage.at[:, part], basis.at[:, part], sem.at[c])

    @pl.loop(0, chunks)
    def _(c):
        @pl.loop(0, planes)
        def _(p):
            x = c * planes + p
            for b in range(ny // 8):
                f = [filtered[o, x, 8 * b : 8 * b + 8, :] for o in range(4)]
                for j in range(4):
                    value = f[0] * w[0, j]
                    for i in range(1, j + 1):
                        value = value + f[i] * w[i, j]
                    stage[j, x, 8 * b : 8 * b + 8, :] = value

        write(c).start()

    @pl.loop(0, chunks)
    def _(c):
        write(c).wait()


def body(orbitals, potential):
    orbs, nx, ny, nz = orbitals.shape
    cx, cy, cz = (lax.axis_size(a) for a in ("gx", "gy", "gz"))
    slabs, groups = nx // SLAB, ny // 32
    dma = pltpu.SemaphoreType.DMA
    f32 = jnp.float32
    filtered, gram = pl.pallas_call(
        functools.partial(filter_kernel, (nx, ny, cx, cy, cz)),
        out_shape=(
            pltpu.VMEM(orbitals.shape, f32),
            pltpu.VMEM((8, LANES), f32),
        ),
        in_specs=[pl.BlockSpec(memory_space=pl.ANY)] * 2,
        out_specs=(
            pl.BlockSpec(memory_space=pltpu.VMEM),
            pl.BlockSpec(memory_space=pltpu.VMEM),
        ),
        scratch_shapes=[
            pltpu.VMEM((2, orbs, nx + 4, ny + 16, nz), f32),
            pltpu.VMEM((nx, ny, nz), f32),
            pltpu.VMEM((orbs // 2, nx, ny, nz), f32),
            pltpu.VMEM((orbs // 2, nx, ny, nz), f32),
            pltpu.VMEM((orbs, SLAB * ny, 2 * nz), jnp.bfloat16),
            pltpu.VMEM((2 * nz, 2 * nz), jnp.bfloat16),
            pltpu.VMEM((3, slabs, orbs, groups, 8, LANES), f32),
            pltpu.VMEM((3, 2, slabs, orbs, groups, 8, LANES), f32),
            pltpu.VMEM((10, 8, LANES), f32),
            pltpu.VMEM((cz, 8, LANES), f32),
            pltpu.VMEM((cx * cy, 8, LANES), f32),
            dma((slabs,)),
            dma((slabs,)),
            dma((3, 2)),
            dma((3, 2)),
            dma((3, 2, slabs)),
            dma((3, 2, slabs)),
            dma((3, 2, slabs)),
            dma((3, 2, slabs)),
            dma((cz,)),
            dma((cz,)),
            dma((cx * cy,)),
            dma((cx * cy,)),
        ],
        compiler_params=pltpu.CompilerParams(
            collective_id=0, has_side_effects=True, vmem_limit_bytes=48 << 20
        ),
    )(orbitals, potential)
    basis, factor = pl.pallas_call(
        functools.partial(basis_kernel, nx * cx * ny * cy * nz * cz),
        out_shape=(
            jax.ShapeDtypeStruct(orbitals.shape, f32),
            jax.ShapeDtypeStruct((4, 4), f32),
        ),
        in_specs=[pl.BlockSpec(memory_space=pltpu.VMEM)] * 2,
        out_specs=(
            pl.BlockSpec(memory_space=pl.ANY),
            pl.BlockSpec(memory_space=pltpu.VMEM),
        ),
        scratch_shapes=[pltpu.VMEM(orbitals.shape, f32), dma((nx // 4,))],
        compiler_params=pltpu.CompilerParams(vmem_limit_bytes=16 << 20),
    )(
        pltpu.with_memory_space_constraint(filtered, pltpu.VMEM),
        pltpu.with_memory_space_constraint(gram, pltpu.VMEM),
    )
    return basis, factor


def solution(mesh):
    return jax.shard_map(
        body,
        mesh=mesh,
        in_specs=(P(None, "gx", "gy", "gz"), P("gx", "gy", "gz")),
        out_specs=(P(None, "gx", "gy", "gz"), P()),
        check_vma=False,
    )
```

```python
import functools

import jax
import jax.numpy as jnp
from jax import lax
from jax.experimental import pallas as pl
from jax.experimental.pallas import tpu as pltpu
from jax.sharding import PartitionSpec as P

MESH = pl.DeviceIdType.MESH
LANES = 128
SLAB = 8
ROW0 = 8


def merge(tree, value, lane):
    size = 0
    while tree and tree[-1][0] == size:
        low = tree.pop()[1]
        value = jnp.where((lane & (4 << size)) != 0, value, low)
        size += 1
    tree.append((size, value))


def halves(rows):
    parts = []
    for k in range(0, len(rows), 2):
        pair = jnp.concatenate(rows[k : k + 2], axis=0)
        high = pair.astype(jnp.bfloat16)
        low = (pair - high.astype(jnp.float32)).astype(jnp.bfloat16)
        parts.append(jnp.concatenate([high, low], axis=1))
    return jnp.concatenate(parts, axis=0)


def filter_kernel(
    sizes, orb, pot, out, gram, u, q, zp, zl, half, weights, own, zin, acc, g0, g1,
    load_sem, pot_sem, xs, xr, ys, yr, zs, zr, g0s, g0r, g1s, g1r,
):
    nx, ny, cx, cy, cz = sizes
    slabs = nx // SLAB
    blocks = ny // 8
    groups = blocks // 4
    orbs = 4
    gx, gy, gz = lax.axis_index("gx"), lax.axis_index("gy"), lax.axis_index("gz")
    here = [gx, gy, gz]
    counts = [cx, cy, cz]

    def device(axis, index):
        return tuple(index if a == axis else here[a] for a in range(3))

    def load(s):
        x0 = s * SLAB
        return (
            pltpu.make_async_copy(
                orb.at[:, pl.ds(x0, SLAB)],
                u.at[0, :, pl.ds(2 + x0, SLAB), pl.ds(ROW0, ny)],
                load_sem.at[s],
            ),
            pltpu.make_async_copy(
                pot.at[pl.ds(x0, SLAB)], q.at[pl.ds(x0, SLAB)], pot_sem.at[s]
            ),
        )

    @pl.loop(0, slabs)
    def _(i):
        for copy in load(lax.rem(i + 1, slabs)):
            copy.start()

    plane = cx * cy
    spot = gx * cy + gy
    far = lambda k, count: -min(k, count - k)
    line = sorted(range(1, cz), key=lambda k: far(k, cz))
    square = sorted(range(1, plane), key=lambda k: far(k // cy, cx) + far(k % cy, cy))

    def line_peer(k, sign):
        return (gx, gy, lax.rem(gz + cz + sign * k, cz))

    def plane_peer(k, sign):
        dx, dy = sign * (k // cy), sign * (k % cy)
        return (lax.rem(gx + cx + dx, cx), lax.rem(gy + cy + dy, cy), gz)

    barrier = pltpu.get_barrier_semaphore()
    for order, peer in ((line, line_peer), (square, plane_peer)):
        for k in order:
            pl.semaphore_signal(
                barrier, inc=1, device_id=peer(k, 1), device_id_type=MESH
            )

    def x_copy(level, side):
        buf = level % 2
        first = nx if side == 0 else 2
        target = 0 if side == 0 else nx + 2
        if level == 0:
            source = orb.at[:, pl.ds(first - 2, 2)]
        else:
            source = u.at[buf, :, pl.ds(first, 2), pl.ds(ROW0, ny)]
        return pltpu.make_async_remote_copy(
            src_ref=source,
            dst_ref=u.at[buf, :, pl.ds(target, 2), pl.ds(ROW0, ny)],
            send_sem=xs.at[level, side],
            recv_sem=xr.at[level, side],
            device_id=device(0, gx + 1 if side == 0 else gx - 1),
            device_id_type=MESH,
        )

    def y_copy(level, side, s):
        buf = level % 2
        planes = pl.ds(2 + s * SLAB, SLAB)
        first = ROW0 + ny - 2 if side == 0 else ROW0
        target = ROW0 - 2 if side == 0 else ROW0 + ny
        return pltpu.make_async_remote_copy(
            src_ref=u.at[buf, :, planes, pl.ds(first, 2)],
            dst_ref=u.at[buf, :, planes, pl.ds(target, 2)],
            send_sem=ys.at[level, side, s],
            recv_sem=yr.at[level, side, s],
            device_id=device(1, gy + 1 if side == 0 else gy - 1),
            device_id_type=MESH,
        )

    def z_copy(level, side, s):
        return pltpu.make_async_remote_copy(
            src_ref=own.at[level, s],
            dst_ref=zin.at[level, side, s],
            send_sem=zs.at[level, side, s],
            recv_sem=zr.at[level, side, s],
            device_id=device(2, gz + 1 if side == 0 else gz - 1),
            device_id_type=MESH,
        )

    def sends(axis, side):
        return here[axis] < counts[axis] - 1 if side == 0 else here[axis] > 0

    def receives(axis, side):
        return here[axis] > 0 if side == 0 else here[axis] < counts[axis] - 1

    def send_rows(level, s):
        for side in range(2):

            @pl.when(sends(1, side))
            def _():
                y_copy(level, side, s).start()

    def send_ends(level, s):
        for side in range(2):

            @pl.when(sends(2, side))
            def _():
                z_copy(level, side, s).start()

    for side in range(2):
        xt = 0 if side == 0 else nx + 2
        yt = ROW0 - 2 if side == 0 else ROW0 + ny

        @pl.when(jnp.logical_not(receives(0, side)))
        def _():
            @pl.loop(0, orbs)
            def _(o):
                for buf in range(2):
                    for plane in range(2):
                        u[buf, o, xt + plane, ROW0 : ROW0 + ny, :] = jnp.zeros(
                            (ny, LANES), jnp.float32
                        )

        @pl.when(jnp.logical_not(receives(1, side)))
        def _():
            @pl.loop(0, orbs)
            def _(o):
                @pl.loop(0, slabs)
                def _(s):
                    for x in range(SLAB):
                        for buf in range(2):
                            u[buf, o, 2 + s * SLAB + x, yt : yt + 2, :] = jnp.zeros(
                                (2, LANES), jnp.float32
                            )

        @pl.when(jnp.logical_not(receives(2, side)))
        def _():
            @pl.loop(0, slabs)
            def _(s):
                for level in range(3):
                    zin[level, side, s] = jnp.zeros((orbs, groups, 8, LANES), jnp.float32)

    lane = lax.broadcasted_iota(jnp.int32, (8, LANES), 1)
    phase = lane & 3
    edge = (lane < 2) | (lane >= LANES - 2)

    source = lax.broadcasted_iota(jnp.int32, (2 * LANES, 2 * LANES), 0) & (LANES - 1)
    target = lax.broadcasted_iota(jnp.int32, (2 * LANES, 2 * LANES), 1)
    step = (target - source) & (LANES - 1)
    band = jnp.where(
        (step == 1) | (step == LANES - 1),
        -16.0,
        jnp.where((step == 2) | (step == LANES - 2), 1.0, 0.0),
    )
    ends = jnp.where((target & 3) == ((source + 2) & (LANES - 1)), 1.0, 0.0)
    weights[...] = jnp.where(target < LANES, band, ends).astype(jnp.bfloat16)

    pl.semaphore_wait(barrier, cz + plane - 2)
    for side in range(2):

        @pl.when(sends(0, side))
        def _():
            x_copy(0, side).start()

    pair = orbs // 2

    def along(o):
        return (zp, o) if o < pair else (zl, o - pair)

    def along_z(level, s, start, count):
        size = SLAB * ny
        done = jnp.dot(
            half[start : start + count].reshape(count * size, 2 * LANES),
            weights[...],
            preferred_element_type=jnp.float32,
        )
        for o in range(start, start + count):
            ref, part = along(o)
            for g in range(groups):
                tree = []
                for b in range(4 * g, 4 * g + 4):
                    for x in range(SLAB):
                        row = (o - start) * size + 8 * (b * SLAB + x)
                        ref[part, s * SLAB + x, 8 * b : 8 * b + 8, :] = done[
                            row : row + 8, :LANES
                        ]
                        merge(tree, done[row : row + 8, LANES:], lane)
                own[level, s, o, g] = tree[0][1]

    def arrive(s):
        for copy in load(s):
            copy.wait()

    def split(s):
        x0 = s * SLAB
        for o in range(orbs):
            for b in range(blocks):
                y = ROW0 + 8 * b
                half[o, SLAB * 8 * b : SLAB * 8 * (b + 1), :] = halves(
                    [u[0, o, x0 + 2 + x, y : y + 8, :] for x in range(SLAB)]
                )

    def scale(s):
        @pl.loop(0, SLAB)
        def _(x):
            q[s * SLAB + x] = 24.0 * q[s * SLAB + x] - 18.0

    arrive(1)
    split(1)
    send_rows(0, 1)
    scale(1)

    @pl.loop(1, slabs)
    def _(before):
        s = lax.rem(before + 1, slabs)
        arrive(s)
        along_z(0, before, 0, orbs)
        split(s)
        send_ends(0, before)
        send_rows(0, s)
        scale(s)

    along_z(0, 0, 0, pair)

    def fixes(level, s, o, g):
        delta = (
            jnp.where(phase < 2, zin[level, 0, s, o, g], zin[level, 1, s, o, g])
            - own[level, s, o, g]
        )
        outer = jnp.where(
            phase < 2, pltpu.roll(delta, LANES - 2, 1), pltpu.roll(delta, 2, 1)
        )
        inner = jnp.where(
            phase == 1,
            pltpu.roll(delta, LANES - 1, 1),
            jnp.where(phase == 2, pltpu.roll(delta, 1, 1), 0.0),
        )
        return outer - 16.0 * inner

    def advance(level, s, o, fix):
        src, dst = level % 2, (level + 1) % 2
        x0 = s * SLAB
        ref, part = along(o)
        for b in range(blocks):
            y = ROW0 + 8 * b
            c = [u[src, o, x0 + j, y : y + 8, :] for j in range(SLAB + 4)]
            news = []
            for x in range(SLAB):
                k = (b % 4) * SLAB + x
                px = x0 + 2 + x

                def row(d):
                    return u[src, o, px, y + d : y + d + 8, :]

                one = (c[x + 1] + c[x + 3]) + (row(-1) + row(1))
                two = (c[x] + c[x + 4]) + (row(-2) + row(2))
                cor = jnp.where(
                    edge, pltpu.roll(fix[b // 4], (2 * LANES - 4 * k - 2) % LANES, 1), 0.0
                )
                total = (
                    q[x0 + x, 8 * b : 8 * b + 8, :] * c[x + 2]
                    + (ref[part, x0 + x, 8 * b : 8 * b + 8, :] + cor)
                    + two
                    - 16.0 * one
                )
                if level == 0:
                    new = total
                elif level == 1:
                    new = total * (1.0 / 3528.0) - u[dst, o, px, y : y + 8, :]
                else:
                    new = total - 0.5 * u[dst, o, px, y : y + 8, :]
                if level < 2:
                    u[dst, o, px, y : y + 8, :] = new
                    news.append(new)
                else:
                    out[o, x0 + x, 8 * b : 8 * b + 8, :] = new
            if level < 2:
                row0 = SLAB * 8 * b
                half[o, row0 : row0 + 8 * SLAB, :] = halves(news)

    acc[...] = jnp.zeros_like(acc)

    for level in range(3):

        @pl.loop(0, slabs)
        def _(i, level=level):
            s = lax.rem(i + 1, slabs)
            x0 = s * SLAB
            for side in range(2):

                @pl.when(receives(1, side))
                def _():
                    y_copy(level, side, s).wait_recv()

                @pl.when(receives(2, side))
                def _():
                    z_copy(level, side, s).wait_recv()

                @pl.when(
                    jnp.logical_and(
                        receives(0, side), s == (0 if side == 0 else slabs - 1)
                    )
                )
                def _():
                    x_copy(level, side).wait_recv()

                if level == 1:

                    @pl.when(sends(1, side))
                    def _():
                        y_copy(0, side, s).wait_send()

            fix = [[fixes(level, s, o, g) for g in range(groups)] for o in range(orbs)]
            if level < 2:
                owner = level + lax.div(i + slabs - 1, slabs)
                along_z(owner, i, pair, pair)
            for o in range(orbs):
                advance(level, s, o, fix[o])
                if level < 2 and o == pair:
                    along_z(level + 1, s, 0, pair)
            if level < 2:
                send_rows(level + 1, s)
                send_ends(owner, i)
                for side in range(2):

                    @pl.when(
                        jnp.logical_and(sends(0, side), s == (slabs - 1 if side == 0 else 0))
                    )
                    def _():
                        x_copy(level + 1, side).start()

            else:
                sums = [None] * 10
                for x in range(SLAB):
                    for b in range(blocks):
                        f = [out[o, x0 + x, 8 * b : 8 * b + 8, :] for o in range(orbs)]
                        n = 0
                        for o in range(orbs):
                            for p in range(o, orbs):
                                term = f[o] * f[p]
                                sums[n] = term if sums[n] is None else sums[n] + term
                                n += 1
                for n in range(10):
                    acc[n] = acc[n] + sums[n]

        if level == 1:
            along_z(2, 0, pair, pair)
            send_ends(2, 0)

    rows = [jnp.sum(acc[n], axis=0, keepdims=True) for n in range(10)]
    first = jnp.concatenate(rows[:8], axis=0)
    second = jnp.concatenate(rows[8:] + [jnp.zeros((6, LANES), jnp.float32)], axis=0)
    half_lanes = LANES // 2
    total = jnp.where(
        lane < half_lanes,
        first + pltpu.roll(first, half_lanes, 1),
        second + pltpu.roll(second, half_lanes, 1),
    )
    stages = (
        (gz, cz, line, line_peer, lambda at: at[2], g0, g0s, g0r),
        (spot, plane, square, plane_peer, lambda at: at[0] * cy + at[1], g1, g1s, g1r),
    )

    def sum_copy(stage, k, arrival):
        me, _, _, peer, index, slots, ss, rs = stage
        slot = slots.at[index(peer(k, -1)) if arrival else me]
        return pltpu.make_async_remote_copy(
            src_ref=slot,
            dst_ref=slot,
            send_sem=ss.at[k],
            recv_sem=rs.at[k],
            device_id=peer(k, 1),
            device_id_type=MESH,
        )

    def sent():
        for level in range(3):
            for side in range(2):

                @pl.when(sends(0, side))
                def _():
                    x_copy(level, side).wait_send()

                @pl.loop(0, slabs)
                def _(s):
                    if level > 0:

                        @pl.when(sends(1, side))
                        def _():
                            y_copy(level, side, s).wait_send()

                    @pl.when(sends(2, side))
                    def _():
                        z_copy(level, side, s).wait_send()

    for stage in stages:
        me, count, order, slots = stage[0], stage[1], stage[2], stage[5]
        slots[me] = total
        for k in order:
            sum_copy(stage, k, False).start()
        if stage is stages[0]:
            sent()
        for k in reversed(order):
            sum_copy(stage, k, True).wait_recv()
        total = slots[0]
        for k in range(1, count):
            total = total + slots[k]
    gram[...] = total
    for stage in stages:
        for k in stage[2]:
            sum_copy(stage, k, False).wait_send()


def basis_kernel(cells, filtered, gram, basis, factor, stage, sem):
    def invert():
        lower = lax.broadcasted_iota(jnp.int32, (8, LANES), 1) < LANES // 2
        sums = [
            jnp.broadcast_to(
                jnp.sum(jnp.where(part, gram[...], 0.0), axis=1, keepdims=True)
                * (1.0 / (42.0 * 42.0 * cells)),
                (8, LANES),
            )
            for part in (lower, jnp.logical_not(lower))
        ]
        g, n = {}, 0
        for i in range(4):
            for j in range(i, 4):
                g[i, j] = sums[n // 8][n % 8 : n % 8 + 1, :]
                n += 1
        r = {}
        for i in range(4):
            for j in range(i, 4):
                value = g[i, j]
                for m in range(i):
                    value = value - r[m, i] * r[m, j]
                r[i, j] = jnp.sqrt(value) if i == j else value / r[i, i]
        w = {}
        for j in range(4):
            w[j, j] = 1.0 / r[j, j]
            for i in range(j - 1, -1, -1):
                value = r[i, i + 1] * w[i + 1, j]
                for m in range(i + 2, j + 1):
                    value = value + r[i, m] * w[m, j]
                w[i, j] = -value / r[i, i]
        line = lax.broadcasted_iota(jnp.int32, (4, 4), 0)
        column = lax.broadcasted_iota(jnp.int32, (4, 4), 1)
        table = jnp.zeros((4, 4), jnp.float32)
        for i in range(4):
            for j in range(i, 4):
                table = jnp.where(
                    (line == i) & (column == j), jnp.broadcast_to(r[i, j][:, :4], (4, 4)), table
                )
        factor[...] = table
        return {at: jnp.broadcast_to(value * (1.0 / 42.0), (8, LANES)) for at, value in w.items()}

    w = invert()
    nx, ny = basis.shape[1], basis.shape[2]
    chunks = sem.shape[0]
    planes = nx // chunks

    def write(c):
        part = pl.ds(c * planes, planes)
        return pltpu.make_async_copy(stage.at[:, part], basis.at[:, part], sem.at[c])

    @pl.loop(0, chunks)
    def _(c):
        @pl.loop(0, planes)
        def _(p):
            x = c * planes + p
            for b in range(ny // 8):
                f = [filtered[o, x, 8 * b : 8 * b + 8, :] for o in range(4)]
                for j in range(4):
                    value = f[0] * w[0, j]
                    for i in range(1, j + 1):
                        value = value + f[i] * w[i, j]
                    stage[j, x, 8 * b : 8 * b + 8, :] = value

        write(c).start()

    @pl.loop(0, chunks)
    def _(c):
        write(c).wait()


def body(orbitals, potential):
    orbs, nx, ny, nz = orbitals.shape
    cx, cy, cz = (lax.axis_size(a) for a in ("gx", "gy", "gz"))
    slabs, groups = nx // SLAB, ny // 32
    dma = pltpu.SemaphoreType.DMA
    f32 = jnp.float32
    filtered, gram = pl.pallas_call(
        functools.partial(filter_kernel, (nx, ny, cx, cy, cz)),
        out_shape=(
            pltpu.VMEM(orbitals.shape, f32),
            pltpu.VMEM((8, LANES), f32),
        ),
        in_specs=[pl.BlockSpec(memory_space=pl.ANY)] * 2,
        out_specs=(
            pl.BlockSpec(memory_space=pltpu.VMEM),
            pl.BlockSpec(memory_space=pltpu.VMEM),
        ),
        scratch_shapes=[
            pltpu.VMEM((2, orbs, nx + 4, ny + 16, nz), f32),
            pltpu.VMEM((nx, ny, nz), f32),
            pltpu.VMEM((orbs // 2, nx, ny, nz), f32),
            pltpu.VMEM((orbs // 2, nx, ny, nz), f32),
            pltpu.VMEM((orbs, SLAB * ny, 2 * nz), jnp.bfloat16),
            pltpu.VMEM((2 * nz, 2 * nz), jnp.bfloat16),
            pltpu.VMEM((3, slabs, orbs, groups, 8, LANES), f32),
            pltpu.VMEM((3, 2, slabs, orbs, groups, 8, LANES), f32),
            pltpu.VMEM((10, 8, LANES), f32),
            pltpu.VMEM((cz, 8, LANES), f32),
            pltpu.VMEM((cx * cy, 8, LANES), f32),
            dma((slabs,)),
            dma((slabs,)),
            dma((3, 2)),
            dma((3, 2)),
            dma((3, 2, slabs)),
            dma((3, 2, slabs)),
            dma((3, 2, slabs)),
            dma((3, 2, slabs)),
            dma((cz,)),
            dma((cz,)),
            dma((cx * cy,)),
            dma((cx * cy,)),
        ],
        compiler_params=pltpu.CompilerParams(
            collective_id=0, has_side_effects=True, vmem_limit_bytes=48 << 20
        ),
    )(orbitals, potential)
    basis, factor = pl.pallas_call(
        functools.partial(basis_kernel, nx * cx * ny * cy * nz * cz),
        out_shape=(
            jax.ShapeDtypeStruct(orbitals.shape, f32),
            jax.ShapeDtypeStruct((4, 4), f32),
        ),
        in_specs=[pl.BlockSpec(memory_space=pltpu.VMEM)] * 2,
        out_specs=(
            pl.BlockSpec(memory_space=pl.ANY),
            pl.BlockSpec(memory_space=pltpu.VMEM),
        ),
        scratch_shapes=[pltpu.VMEM(orbitals.shape, f32), dma((nx // 4,))],
        compiler_params=pltpu.CompilerParams(vmem_limit_bytes=16 << 20),
    )(
        pltpu.with_memory_space_constraint(filtered, pltpu.VMEM),
        pltpu.with_memory_space_constraint(gram, pltpu.VMEM),
    )
    return basis, factor


def solution(mesh):
    return jax.shard_map(
        body,
        mesh=mesh,
        in_specs=(P(None, "gx", "gy", "gz"), P("gx", "gy", "gz")),
        out_specs=(P(None, "gx", "gy", "gz"), P()),
        check_vma=False,
    )
```

```python
import functools

import jax
import jax.numpy as jnp
from jax import lax
from jax.experimental import pallas as pl
from jax.experimental.pallas import tpu as pltpu
from jax.sharding import PartitionSpec as P

MESH = pl.DeviceIdType.MESH
LANES = 128
SLAB = 8
ROW0 = 8


def merge(tree, value, lane):
    size = 0
    while tree and tree[-1][0] == size:
        low = tree.pop()[1]
        value = jnp.where((lane & (4 << size)) != 0, value, low)
        size += 1
    tree.append((size, value))


def halves(rows):
    parts = []
    for k in range(0, len(rows), 2):
        pair = jnp.concatenate(rows[k : k + 2], axis=0)
        high = pair.astype(jnp.bfloat16)
        low = (pair - high.astype(jnp.float32)).astype(jnp.bfloat16)
        parts.append(jnp.concatenate([high, low], axis=1))
    return jnp.concatenate(parts, axis=0)


def filter_kernel(
    sizes, orb, pot, out, gram, u, q, zp, zl, half, weights, own, zin, acc, g0, g1,
    load_sem, pot_sem, xs, xr, ys, yr, zs, zr, g0s, g0r, g1s, g1r,
):
    nx, ny, cx, cy, cz = sizes
    slabs = nx // SLAB
    blocks = ny // 8
    groups = blocks // 4
    orbs = 4
    gx, gy, gz = lax.axis_index("gx"), lax.axis_index("gy"), lax.axis_index("gz")
    here = [gx, gy, gz]
    counts = [cx, cy, cz]

    def device(axis, index):
        return tuple(index if a == axis else here[a] for a in range(3))

    def load(s):
        x0 = s * SLAB
        return (
            pltpu.make_async_copy(
                orb.at[:, pl.ds(x0, SLAB)],
                u.at[0, :, pl.ds(2 + x0, SLAB), pl.ds(ROW0, ny)],
                load_sem.at[s],
            ),
            pltpu.make_async_copy(
                pot.at[pl.ds(x0, SLAB)], q.at[pl.ds(x0, SLAB)], pot_sem.at[s]
            ),
        )

    @pl.loop(0, slabs)
    def _(i):
        for copy in load(lax.rem(i + 1, slabs)):
            copy.start()

    plane = cx * cy
    spot = gx * cy + gy
    far = lambda k, count: -min(k, count - k)
    line = sorted(range(1, cz), key=lambda k: far(k, cz))
    square = sorted(range(1, plane), key=lambda k: far(k // cy, cx) + far(k % cy, cy))

    def line_peer(k, sign):
        return (gx, gy, lax.rem(gz + cz + sign * k, cz))

    def plane_peer(k, sign):
        dx, dy = sign * (k // cy), sign * (k % cy)
        return (lax.rem(gx + cx + dx, cx), lax.rem(gy + cy + dy, cy), gz)

    barrier = pltpu.get_barrier_semaphore()
    for order, peer in ((line, line_peer), (square, plane_peer)):
        for k in order:
            pl.semaphore_signal(
                barrier, inc=1, device_id=peer(k, 1), device_id_type=MESH
            )

    def x_copy(level, side):
        buf = level % 2
        first = nx if side == 0 else 2
        target = 0 if side == 0 else nx + 2
        if level == 0:
            source = orb.at[:, pl.ds(first - 2, 2)]
        else:
            source = u.at[buf, :, pl.ds(first, 2), pl.ds(ROW0, ny)]
        return pltpu.make_async_remote_copy(
            src_ref=source,
            dst_ref=u.at[buf, :, pl.ds(target, 2), pl.ds(ROW0, ny)],
            send_sem=xs.at[level, side],
            recv_sem=xr.at[level, side],
            device_id=device(0, gx + 1 if side == 0 else gx - 1),
            device_id_type=MESH,
        )

    def y_copy(level, side, s):
        buf = level % 2
        planes = pl.ds(2 + s * SLAB, SLAB)
        first = ROW0 + ny - 2 if side == 0 else ROW0
        target = ROW0 - 2 if side == 0 else ROW0 + ny
        return pltpu.make_async_remote_copy(
            src_ref=u.at[buf, :, planes, pl.ds(first, 2)],
            dst_ref=u.at[buf, :, planes, pl.ds(target, 2)],
            send_sem=ys.at[level, side, s],
            recv_sem=yr.at[level, side, s],
            device_id=device(1, gy + 1 if side == 0 else gy - 1),
            device_id_type=MESH,
        )

    def z_copy(level, side, s):
        return pltpu.make_async_remote_copy(
            src_ref=own.at[level, s],
            dst_ref=zin.at[level, side, s],
            send_sem=zs.at[level, side, s],
            recv_sem=zr.at[level, side, s],
            device_id=device(2, gz + 1 if side == 0 else gz - 1),
            device_id_type=MESH,
        )

    def sends(axis, side):
        return here[axis] < counts[axis] - 1 if side == 0 else here[axis] > 0

    def receives(axis, side):
        return here[axis] > 0 if side == 0 else here[axis] < counts[axis] - 1

    def send_rows(level, s):
        for side in range(2):

            @pl.when(sends(1, side))
            def _():
                y_copy(level, side, s).start()

    def send_ends(level, s):
        for side in range(2):

            @pl.when(sends(2, side))
            def _():
                z_copy(level, side, s).start()

    for side in range(2):
        xt = 0 if side == 0 else nx + 2
        yt = ROW0 - 2 if side == 0 else ROW0 + ny

        @pl.when(jnp.logical_not(receives(0, side)))
        def _():
            @pl.loop(0, orbs)
            def _(o):
                for buf in range(2):
                    for plane in range(2):
                        u[buf, o, xt + plane, ROW0 : ROW0 + ny, :] = jnp.zeros(
                            (ny, LANES), jnp.float32
                        )

        @pl.when(jnp.logical_not(receives(1, side)))
        def _():
            @pl.loop(0, orbs)
            def _(o):
                @pl.loop(0, slabs)
                def _(s):
                    for x in range(SLAB):
                        for buf in range(2):
                            u[buf, o, 2 + s * SLAB + x, yt : yt + 2, :] = jnp.zeros(
                                (2, LANES), jnp.float32
                            )

        @pl.when(jnp.logical_not(receives(2, side)))
        def _():
            @pl.loop(0, slabs)
            def _(s):
                for level in range(3):
                    zin[level, side, s] = jnp.zeros((orbs, groups, 8, LANES), jnp.float32)

    lane = lax.broadcasted_iota(jnp.int32, (8, LANES), 1)
    phase = lane & 3
    edge = (lane < 2) | (lane >= LANES - 2)

    source = lax.broadcasted_iota(jnp.int32, (2 * LANES, 2 * LANES), 0) & (LANES - 1)
    target = lax.broadcasted_iota(jnp.int32, (2 * LANES, 2 * LANES), 1)
    step = (target - source) & (LANES - 1)
    band = jnp.where(
        (step == 1) | (step == LANES - 1),
        -16.0,
        jnp.where((step == 2) | (step == LANES - 2), 1.0, 0.0),
    )
    ends = jnp.where((target & 3) == ((source + 2) & (LANES - 1)), 1.0, 0.0)
    weights[...] = jnp.where(target < LANES, band, ends).astype(jnp.bfloat16)

    pl.semaphore_wait(barrier, cz + plane - 2)
    for side in range(2):

        @pl.when(sends(0, side))
        def _():
            x_copy(0, side).start()

    pair = orbs // 2

    def along(o):
        return (zp, o) if o < pair else (zl, o - pair)

    def along_z(level, s, start, count):
        size = SLAB * ny
        done = jnp.dot(
            half[start : start + count].reshape(count * size, 2 * LANES),
            weights[...],
            preferred_element_type=jnp.float32,
        )
        for o in range(start, start + count):
            ref, part = along(o)
            for g in range(groups):
                tree = []
                for b in range(4 * g, 4 * g + 4):
                    for x in range(SLAB):
                        row = (o - start) * size + 8 * (b * SLAB + x)
                        ref[part, s * SLAB + x, 8 * b : 8 * b + 8, :] = done[
                            row : row + 8, :LANES
                        ]
                        merge(tree, done[row : row + 8, LANES:], lane)
                own[level, s, o, g] = tree[0][1]

    def arrive(s):
        for copy in load(s):
            copy.wait()

    def split(s):
        x0 = s * SLAB
        for o in range(orbs):
            for b in range(blocks):
                y = ROW0 + 8 * b
                half[o, SLAB * 8 * b : SLAB * 8 * (b + 1), :] = halves(
                    [u[0, o, x0 + 2 + x, y : y + 8, :] for x in range(SLAB)]
                )

    def scale(s):
        @pl.loop(0, SLAB)
        def _(x):
            q[s * SLAB + x] = 24.0 * q[s * SLAB + x] - 18.0

    arrive(1)
    split(1)
    send_rows(0, 1)
    scale(1)

    @pl.loop(1, slabs)
    def _(before):
        s = lax.rem(before + 1, slabs)
        arrive(s)
        along_z(0, before, 0, orbs)
        split(s)
        send_ends(0, before)
        send_rows(0, s)
        scale(s)

    along_z(0, 0, 0, pair)

    def fixes(level, s, o, g):
        delta = (
            jnp.where(phase < 2, zin[level, 0, s, o, g], zin[level, 1, s, o, g])
            - own[level, s, o, g]
        )
        outer = jnp.where(
            phase < 2, pltpu.roll(delta, LANES - 2, 1), pltpu.roll(delta, 2, 1)
        )
        inner = jnp.where(
            phase == 1,
            pltpu.roll(delta, LANES - 1, 1),
            jnp.where(phase == 2, pltpu.roll(delta, 1, 1), 0.0),
        )
        return outer - 16.0 * inner

    def advance(level, s, o, fix):
        src, dst = level % 2, (level + 1) % 2
        x0 = s * SLAB
        ref, part = along(o)
        for b in range(blocks):
            y = ROW0 + 8 * b
            c = [u[src, o, x0 + j, y : y + 8, :] for j in range(SLAB + 4)]
            news = []
            for x in range(SLAB):
                k = (b % 4) * SLAB + x
                px = x0 + 2 + x

                def row(d):
                    return u[src, o, px, y + d : y + d + 8, :]

                one = (c[x + 1] + c[x + 3]) + (row(-1) + row(1))
                two = (c[x] + c[x + 4]) + (row(-2) + row(2))
                cor = jnp.where(
                    edge, pltpu.roll(fix[b // 4], (2 * LANES - 4 * k - 2) % LANES, 1), 0.0
                )
                total = (
                    q[x0 + x, 8 * b : 8 * b + 8, :] * c[x + 2]
                    + (ref[part, x0 + x, 8 * b : 8 * b + 8, :] + cor)
                    + two
                    - 16.0 * one
                )
                if level == 0:
                    new = total
                elif level == 1:
                    new = total * (1.0 / 3528.0) - u[dst, o, px, y : y + 8, :]
                else:
                    new = total - 0.5 * u[dst, o, px, y : y + 8, :]
                if level < 2:
                    u[dst, o, px, y : y + 8, :] = new
                    news.append(new)
                else:
                    out[o, x0 + x, 8 * b : 8 * b + 8, :] = new
            if level < 2:
                row0 = SLAB * 8 * b
                half[o, row0 : row0 + 8 * SLAB, :] = halves(news)

    acc[...] = jnp.zeros_like(acc)

    for level in range(3):

        @pl.loop(0, slabs)
        def _(i, level=level):
            s = lax.rem(i + 1, slabs)
            x0 = s * SLAB
            for side in range(2):

                @pl.when(receives(1, side))
                def _():
                    y_copy(level, side, s).wait_recv()

                @pl.when(receives(2, side))
                def _():
                    z_copy(level, side, s).wait_recv()

                @pl.when(
                    jnp.logical_and(
                        receives(0, side), s == (0 if side == 0 else slabs - 1)
                    )
                )
                def _():
                    x_copy(level, side).wait_recv()

                if level == 1:

                    @pl.when(sends(1, side))
                    def _():
                        y_copy(0, side, s).wait_send()

            fix = [[fixes(level, s, o, g) for g in range(groups)] for o in range(orbs)]
            if level < 2:
                owner = level + lax.div(i + slabs - 1, slabs)
                along_z(owner, i, pair, pair)
            for o in range(orbs):
                advance(level, s, o, fix[o])
                if level < 2 and o == pair:
                    along_z(level + 1, s, 0, pair)
            if level < 2:
                send_rows(level + 1, s)
                send_ends(owner, i)
                for side in range(2):

                    @pl.when(
                        jnp.logical_and(sends(0, side), s == (slabs - 1 if side == 0 else 0))
                    )
                    def _():
                        x_copy(level + 1, side).start()

            else:
                sums = [None] * 10
                for x in range(SLAB):
                    for b in range(blocks):
                        f = [out[o, x0 + x, 8 * b : 8 * b + 8, :] for o in range(orbs)]
                        n = 0
                        for o in range(orbs):
                            for p in range(o, orbs):
                                term = f[o] * f[p]
                                sums[n] = term if sums[n] is None else sums[n] + term
                                n += 1
                for n in range(10):
                    acc[n] = acc[n] + sums[n]

        if level == 1:
            along_z(2, 0, pair, pair)
            send_ends(2, 0)

    rows = [jnp.sum(acc[n], axis=0, keepdims=True) for n in range(10)]
    first = jnp.concatenate(rows[:8], axis=0)
    second = jnp.concatenate(rows[8:] + [jnp.zeros((6, LANES), jnp.float32)], axis=0)
    half_lanes = LANES // 2
    total = jnp.where(
        lane < half_lanes,
        first + pltpu.roll(first, half_lanes, 1),
        second + pltpu.roll(second, half_lanes, 1),
    )
    stages = (
        (gz, cz, line, line_peer, lambda at: at[2], g0, g0s, g0r),
        (spot, plane, square, plane_peer, lambda at: at[0] * cy + at[1], g1, g1s, g1r),
    )

    def sum_copy(stage, k, arrival):
        me, _, _, peer, index, slots, ss, rs = stage
        slot = slots.at[index(peer(k, -1)) if arrival else me]
        return pltpu.make_async_remote_copy(
            src_ref=slot,
            dst_ref=slot,
            send_sem=ss.at[k],
            recv_sem=rs.at[k],
            device_id=peer(k, 1),
            device_id_type=MESH,
        )

    def sent():
        for level in range(3):
            for side in range(2):

                @pl.when(sends(0, side))
                def _():
                    x_copy(level, side).wait_send()

                @pl.loop(0, slabs)
                def _(s):
                    if level > 0:

                        @pl.when(sends(1, side))
                        def _():
                            y_copy(level, side, s).wait_send()

                    @pl.when(sends(2, side))
                    def _():
                        z_copy(level, side, s).wait_send()

    for stage in stages:
        me, count, order, slots = stage[0], stage[1], stage[2], stage[5]
        slots[me] = total
        for k in order:
            sum_copy(stage, k, False).start()
        if stage is stages[0]:
            sent()
        for k in reversed(order):
            sum_copy(stage, k, True).wait_recv()
        total = slots[0]
        for k in range(1, count):
            total = total + slots[k]
    gram[...] = total
    for stage in stages:
        for k in stage[2]:
            sum_copy(stage, k, False).wait_send()


def basis_kernel(cells, filtered, gram, basis, factor, stage, sem):
    def invert():
        lower = lax.broadcasted_iota(jnp.int32, (8, LANES), 1) < LANES // 2
        sums = [
            jnp.broadcast_to(
                jnp.sum(jnp.where(part, gram[...], 0.0), axis=1, keepdims=True)
                * (1.0 / (42.0 * 42.0 * cells)),
                (8, LANES),
            )
            for part in (lower, jnp.logical_not(lower))
        ]
        g, n = {}, 0
        for i in range(4):
            for j in range(i, 4):
                g[i, j] = sums[n // 8][n % 8 : n % 8 + 1, :]
                n += 1
        r, over = {}, {}
        for i in range(4):
            for j in range(i, 4):
                value = g[i, j]
                for m in range(i):
                    value = value - r[m, i] * r[m, j]
                if i == j:
                    r[i, i] = jnp.sqrt(value)
                    over[i] = 1.0 / r[i, i]
                else:
                    r[i, j] = value * over[i]
        w = {}
        for j in range(4):
            w[j, j] = over[j]
            for i in range(j - 1, -1, -1):
                value = r[i, i + 1] * w[i + 1, j]
                for m in range(i + 2, j + 1):
                    value = value + r[i, m] * w[m, j]
                w[i, j] = -value * over[i]
        line = lax.broadcasted_iota(jnp.int32, (4, 4), 0)
        column = lax.broadcasted_iota(jnp.int32, (4, 4), 1)
        table = jnp.zeros((4, 4), jnp.float32)
        for i in range(4):
            for j in range(i, 4):
                table = jnp.where(
                    (line == i) & (column == j), jnp.broadcast_to(r[i, j][:, :4], (4, 4)), table
                )
        factor[...] = table
        return {at: jnp.broadcast_to(value * (1.0 / 42.0), (8, LANES)) for at, value in w.items()}

    w = invert()
    nx, ny = basis.shape[1], basis.shape[2]
    chunks = sem.shape[0]
    planes = nx // chunks

    def write(c):
        part = pl.ds(c * planes, planes)
        return pltpu.make_async_copy(stage.at[:, part], basis.at[:, part], sem.at[c])

    @pl.loop(0, chunks)
    def _(c):
        @pl.loop(0, planes)
        def _(p):
            x = c * planes + p
            for b in range(ny // 8):
                f = [filtered[o, x, 8 * b : 8 * b + 8, :] for o in range(4)]
                for j in range(4):
                    value = f[0] * w[0, j]
                    for i in range(1, j + 1):
                        value = value + f[i] * w[i, j]
                    stage[j, x, 8 * b : 8 * b + 8, :] = value

        write(c).start()

    @pl.loop(0, chunks)
    def _(c):
        write(c).wait()


def body(orbitals, potential):
    orbs, nx, ny, nz = orbitals.shape
    cx, cy, cz = (lax.axis_size(a) for a in ("gx", "gy", "gz"))
    slabs, groups = nx // SLAB, ny // 32
    dma = pltpu.SemaphoreType.DMA
    f32 = jnp.float32
    filtered, gram = pl.pallas_call(
        functools.partial(filter_kernel, (nx, ny, cx, cy, cz)),
        out_shape=(
            pltpu.VMEM(orbitals.shape, f32),
            pltpu.VMEM((8, LANES), f32),
        ),
        in_specs=[pl.BlockSpec(memory_space=pl.ANY)] * 2,
        out_specs=(
            pl.BlockSpec(memory_space=pltpu.VMEM),
            pl.BlockSpec(memory_space=pltpu.VMEM),
        ),
        scratch_shapes=[
            pltpu.VMEM((2, orbs, nx + 4, ny + 16, nz), f32),
            pltpu.VMEM((nx, ny, nz), f32),
            pltpu.VMEM((orbs // 2, nx, ny, nz), f32),
            pltpu.VMEM((orbs // 2, nx, ny, nz), f32),
            pltpu.VMEM((orbs, SLAB * ny, 2 * nz), jnp.bfloat16),
            pltpu.VMEM((2 * nz, 2 * nz), jnp.bfloat16),
            pltpu.VMEM((3, slabs, orbs, groups, 8, LANES), f32),
            pltpu.VMEM((3, 2, slabs, orbs, groups, 8, LANES), f32),
            pltpu.VMEM((10, 8, LANES), f32),
            pltpu.VMEM((cz, 8, LANES), f32),
            pltpu.VMEM((cx * cy, 8, LANES), f32),
            dma((slabs,)),
            dma((slabs,)),
            dma((3, 2)),
            dma((3, 2)),
            dma((3, 2, slabs)),
            dma((3, 2, slabs)),
            dma((3, 2, slabs)),
            dma((3, 2, slabs)),
            dma((cz,)),
            dma((cz,)),
            dma((cx * cy,)),
            dma((cx * cy,)),
        ],
        compiler_params=pltpu.CompilerParams(
            collective_id=0, has_side_effects=True, vmem_limit_bytes=48 << 20
        ),
    )(orbitals, potential)
    basis, factor = pl.pallas_call(
        functools.partial(basis_kernel, nx * cx * ny * cy * nz * cz),
        out_shape=(
            jax.ShapeDtypeStruct(orbitals.shape, f32),
            jax.ShapeDtypeStruct((4, 4), f32),
        ),
        in_specs=[pl.BlockSpec(memory_space=pltpu.VMEM)] * 2,
        out_specs=(
            pl.BlockSpec(memory_space=pl.ANY),
            pl.BlockSpec(memory_space=pltpu.VMEM),
        ),
        scratch_shapes=[pltpu.VMEM(orbitals.shape, f32), dma((nx // 4,))],
        compiler_params=pltpu.CompilerParams(vmem_limit_bytes=16 << 20),
    )(
        pltpu.with_memory_space_constraint(filtered, pltpu.VMEM),
        pltpu.with_memory_space_constraint(gram, pltpu.VMEM),
    )
    return basis, factor


def solution(mesh):
    return jax.shard_map(
        body,
        mesh=mesh,
        in_specs=(P(None, "gx", "gy", "gz"), P("gx", "gy", "gz")),
        out_specs=(P(None, "gx", "gy", "gz"), P()),
        check_vma=False,
    )
```
